32 devices in a mesh: seq: 8 (over z, core), chan: 4 (over y, x).
Axes of the slice: x: 2, y: 2, z: 4, core: 2. Of those that a mesh axis runs over, the one named last changes fastest.
Arguments:
- query_proj: bfloat16 [1024, 16384], P('chan', 'seq'), may hold values from -6 to 6
- key_proj: bfloat16 [1024, 16384], P('chan', 'seq'), may hold values from -6 to 6
- value_proj: bfloat16 [1024, 16384], P('chan', 'seq'), may hold values from -6 to 6
- short_taps: bfloat16 [3, 7, 1024], P(None, None, 'chan'), may hold values from -2 to 2
- skip_gain: float32 [1024], P('chan'), may hold values from 0.5 to 1.5
- filter_raw: bfloat16 [1024, 16384], P(None, ('seq', 'chan')), may hold values from -6 to 6
- grad_out: bfloat16 [1024, 16384], P('chan', 'seq'), may hold values from -6 to 6
Outputs:
- mixed_out: bfloat16 [1024, 16384], P('chan', 'seq')
- grad_query: bfloat16 [1024, 16384], P('chan', 'seq')
- grad_key: bfloat16 [1024, 16384], P('chan', 'seq')
- grad_value: bfloat16 [1024, 16384], P('chan', 'seq')
- grad_short: float32 [3, 7, 1024], P(None, None, 'chan')
- grad_skip: float32 [1024], P('chan')
- grad_filter: bfloat16 [1024, 16384], P(None, ('seq', 'chan'))
The draws below stay inside these ranges and needn't reach their ends.
All inputs are finite; a program needn't handle non-finite values.
Results may differ from the reference program's by a relative error of at most 0.013.
Values may be sent and summed in bfloat16 or wider, within the bound.
A program may use at most 192 MiB of HBM per device.

```python
import math
import jax
import jax.numpy as jnp
from jax import lax

C = 1024
SHORT = 7
L = 16384


def steps_of(key, extent, cuts, smallest, top_value):
    loudness, own = 1.0, jax.random.fold_in(key, 6)
    for axis_at, parts in cuts:
        heights = jnp.exp(jax.random.uniform(jax.random.fold_in(own, axis_at), (parts,), jnp.float32, smallest / len(cuts), top_value / len(cuts)))
        loudness = loudness * jnp.repeat(heights, extent[axis_at] // parts).reshape([-1 if axis == axis_at else 1 for axis in range(len(extent))])
    return loudness


def noise(own_key, extent, width, most, split=(), held_as=jnp.bfloat16):
    array = jax.random.normal(own_key, extent, jnp.float32) * width
    if len(split) > 0:
        array = steps_of(own_key, extent, split, -0.22, 0.18) * array
    return jnp.clip(array, min=-most, max=most).astype(held_as)


def setup_inputs(seed: int = 0) -> dict:
    splits = jax.random.split(jax.random.key(seed), 8)
    return {
        "query_proj": noise(splits[0], (C, L), 1.0, 6.0, ((0, 4), (1, 8))),
        "key_proj": noise(splits[1], (C, L), 1.0, 6.0, ((0, 4), (1, 8))),
        "value_proj": noise(splits[2], (C, L), 1.0, 6.0, ((0, 4), (1, 8))),
        "short_taps": noise(splits[3], (3, SHORT, C), SHORT ** -0.5, 2.0, ((2, 4),)),
        "skip_gain": jnp.clip(0.5 + 1.0 * jax.random.uniform(splits[4], (C,), jnp.float32) ** steps_of(splits[4], (C,), ((0, 4),), -0.2, 0.2), 0.5, 1.5),
        "filter_raw": noise(splits[5], (C, L), 1.0, 6.0, ((1, 32),)),
        "grad_out": noise(splits[6], (C, L), 1.0, 6.0, ((0, 4), (1, 8))),
    }


def short_causal(padded, taps):
    span = taps.shape[1]
    length = padded.shape[-1] - (span - 1)
    running = jnp.zeros(padded.shape[:-1] + (length,), jnp.float32)
    for offset in range(span):
        begin_at = span - 1 - offset
        running = running + taps[:, offset, :, None].astype(jnp.float32) * padded[..., begin_at:begin_at + length].astype(jnp.float32)
    return running

def short_anticausal(padded, taps):
    span = taps.shape[1]
    length = padded.shape[-1] - (span - 1)
    running = jnp.zeros(padded.shape[:-1] + (length,), jnp.float32)
    for offset in range(span):
        running = running + taps[:, offset, :, None].astype(jnp.float32) * padded[..., offset:offset + length].astype(jnp.float32)
    return running

def short_grads(grad_feats, padded_in):
    span = padded_in.shape[-1] - grad_feats.shape[-1] + 1
    length = grad_feats.shape[-1]
    columns = []
    for offset in range(span):
        begin_at = span - 1 - offset
        columns.append(lax.optimization_barrier(jnp.sum(grad_feats.astype(jnp.float32) * padded_in[..., begin_at:begin_at + length].astype(jnp.float32), axis=-1)))
    return jnp.stack(columns, axis=1)

def causal_long(kernel, signal):
    length = signal.shape[1]
    spectra = jnp.fft.rfft(kernel, n=2 * length, axis=1) * jnp.fft.rfft(signal, n=2 * length, axis=1)
    return jnp.fft.irfft(spectra, n=2 * length, axis=1)[:, :length]

def correlate_long(first, second):
    length = second.shape[1]
    spectra = jnp.conj(jnp.fft.rfft(first, n=2 * length, axis=1)) * jnp.fft.rfft(second, n=2 * length, axis=1)
    return jnp.fft.irfft(spectra, n=2 * length, axis=1)[:, :length]

def reference(query_proj, key_proj, value_proj, short_taps, skip_gain, filter_raw, grad_out):
    length = query_proj.shape[1]
    scale_root = 1.0 / math.sqrt(length)
    span = short_taps.shape[1]
    stacked = jnp.stack([query_proj, key_proj, value_proj])
    padded_in = jnp.pad(stacked, ((0, 0), (0, 0), (span - 1, 0)))
    features = short_causal(padded_in, short_taps)
    queries_short = features[0].astype(jnp.bfloat16)
    mixer_in = (features[1] * features[2]).astype(jnp.bfloat16)
    kernel = filter_raw.astype(jnp.float32) * scale_root
    mixer_float = mixer_in.astype(jnp.float32)
    long_out = causal_long(kernel, mixer_float).astype(jnp.bfloat16)
    gate_arg = long_out.astype(jnp.float32) + skip_gain[:, None] * mixer_float
    mixed_out = (queries_short.astype(jnp.float32) * gate_arg).astype(jnp.bfloat16)
    grad_float = grad_out.astype(jnp.float32)
    inner_grad = grad_float * queries_short.astype(jnp.float32)
    grad_query_short = grad_float * gate_arg
    grad_long = inner_grad.astype(jnp.bfloat16).astype(jnp.float32)
    back_mix = correlate_long(kernel, grad_long).astype(jnp.bfloat16)
    grad_filter = (correlate_long(mixer_float, grad_long) * scale_root).astype(jnp.bfloat16)
    grad_mix = (back_mix.astype(jnp.float32) + skip_gain[:, None] * inner_grad).astype(jnp.bfloat16)
    grad_skip = lax.optimization_barrier(jnp.sum(inner_grad * mixer_float, axis=1)) * scale_root
    grad_mix_float = grad_mix.astype(jnp.float32)
    grad_feats = jnp.stack([grad_query_short, grad_mix_float * features[2], grad_mix_float * features[1]]).astype(jnp.bfloat16)
    padded_grad = jnp.pad(grad_feats, ((0, 0), (0, 0), (0, span - 1)))
    grads_in = short_anticausal(padded_grad, short_taps).astype(jnp.bfloat16)
    grad_short = short_grads(grad_feats, padded_in) * scale_root
    return (mixed_out, grads_in[0], grads_in[1], grads_in[2], grad_short, grad_skip, grad_filter)
```

```python
import functools
import math

import jax
import jax.numpy as jnp
import numpy as np
from jax import lax
from jax.experimental import pallas as pl
from jax.experimental.pallas import tpu as pltpu
from jax.sharding import PartitionSpec as P
import ml_dtypes

MESH = pl.DeviceIdType.MESH
F32 = jnp.float32
BF16 = jnp.bfloat16
LANES = 128


def make_tables(length):
    points = 2 * length
    rows = points // LANES
    half = rows // 2
    n1 = np.arange(half, dtype=np.float64)
    k1 = np.arange(half, dtype=np.float64) + 0.5
    n2 = np.arange(LANES, dtype=np.float64)
    angle = 2 * np.pi * np.outer(k1, n1) / rows
    first = np.concatenate([np.cos(angle), -np.sin(angle)], axis=0)
    last = np.concatenate([np.cos(angle.T), -np.sin(angle.T)], axis=1)
    angle = 2 * np.pi * np.outer(n2, n2) / LANES
    c, s = np.cos(angle), np.sin(angle)
    cols = np.block([[c, -s], [s, c]])
    cols_back = np.block([[c, s], [-s, c]])
    angle = 2 * np.pi * np.outer(k1, n2) / points
    scale = (2.0 / points) / math.sqrt(length)
    twist = np.stack([np.cos(angle), np.sin(angle)])
    as16 = lambda a: jnp.asarray(a.astype(np.float32).astype(ml_dtypes.bfloat16))
    as32 = lambda a: jnp.asarray(a.astype(np.float32))
    return as16(first), as16(last), as16(cols), as16(cols_back), as32(twist), as32(twist * scale)


def kernel(
    dims,
    q_hbm, k_hbm, v_hbm, g_hbm, taps_ref, skip_ref, filt_hbm,
    first_ref, last_ref, cols_ref, cols_back_ref, twist_ref, twist_back_ref,
    mixed_hbm, gq_hbm, gk_hbm, gv_hbm, short_out, skip_out, gf_hbm,
    q, k, v, g, tab_t, tab, part, qs, feat1, feat2,
    halo_send, halo_recv, x_send, g_send, filt_recv, x_recv, g_recv,
    rt, spec_k, spec_x, spec_g, y_send, b_send, f_send, y_recv, b_recv,
    gf0, gf1, gf2, mixed, gq, gk, gv, sums_send, sums_recv,
    in_sem, out_sem, own_sem, halo_ssem, halo_rsem, ssem, rsem,
):
    S, H, G, T, FT = dims
    half = S * T // LANES
    rb = min(16, G)
    W = min(512, T)
    chunks = T // W
    ndev = S * H
    me_s = lax.axis_index("seq")
    me_c = lax.axis_index("chan")
    me = me_s * H + me_c
    scale_root = 1.0 / math.sqrt(S * T)

    ins = [
        pltpu.make_async_copy(src, dst, in_sem.at[i])
        for i, (src, dst) in enumerate(((q_hbm, q), (k_hbm, k), (v_hbm, v), (g_hbm, g)))
    ]
    for copy in ins:
        copy.start()
    barrier = pltpu.get_barrier_semaphore()

    @pl.loop(1, ndev)
    def _(d):
        t = lax.rem(me + d, ndev)
        pl.semaphore_signal(
            barrier, inc=1, device_id=(t // H, lax.rem(t, H)), device_id_type=MESH
        )

    tab_t[...] = jnp.zeros_like(tab_t)
    for i in range(3):
        tab_t[8 * i : 8 * i + 7, :] = taps_ref[i].astype(F32)
    tab_t[7:8, :] = skip_ref[...]
    tab[...] = jnp.transpose(tab_t[...]).reshape(tab.shape)

    lane = lax.broadcasted_iota(jnp.int32, (rb, LANES), 1)
    for copy in ins[:3]:
        copy.wait()

    @pl.loop(0, S)
    def _(grp):
        for sb in range(G // rb):
            rows = slice(sb * rb, sb * rb + rb)
            tails = [r[grp, rows, T - LANES : T].astype(F32) for r in (q, k, v)]
            packed = jnp.where(
                lane >= 122,
                tails[0],
                jnp.where(
                    lane >= 116,
                    pltpu.roll(tails[1], LANES - 6, 1),
                    pltpu.roll(tails[2], LANES - 12, 1),
                ),
            )
            halo_send[0, grp, rows, :] = packed.astype(BF16)

    pl.semaphore_wait(barrier, ndev - 1)

    def halo_copy(which, step):
        target = lax.rem(me_s + step + S, S)
        return pltpu.make_async_remote_copy(
            src_ref=halo_send.at[which], dst_ref=halo_recv.at[which],
            send_sem=halo_ssem.at[which], recv_sem=halo_rsem.at[which],
            device_id=(target, me_c), device_id_type=MESH,
        )

    @pl.when(me_s < S - 1)
    def _():
        halo_copy(0, 1).start()

    @pl.loop(1, ndev)
    def _(d):
        t = lax.rem(me + d, ndev)
        ts, tc = t // H, lax.rem(t, H)
        pltpu.make_async_remote_copy(
            src_ref=filt_hbm.at[tc * S + ts], dst_ref=filt_recv.at[me],
            send_sem=ssem.at[0], recv_sem=rsem.at[0],
            device_id=(ts, tc), device_id_type=MESH,
        ).start()

    own_filter = pltpu.make_async_copy(
        filt_hbm.at[me_c * S + me_s], filt_recv.at[me], own_sem.at[0]
    )
    own_filter.start()
    ins[3].wait()

    @pl.when(me_s > 0)
    def _():
        halo_copy(0, -1).wait_recv()

    @pl.when(me_s == 0)
    def _():
        halo_recv[0] = jnp.zeros(halo_recv.shape[1:], BF16)

    def column(table, i, j):
        return table[:, 8 * i + j : 8 * i + j + 1]

    def exchange(n, send, recv, grp):
        return pltpu.make_async_remote_copy(
            src_ref=send.at[grp], dst_ref=recv.at[me_s],
            send_sem=ssem.at[n], recv_sem=rsem.at[n],
            device_id=(grp, me_c), device_id_type=MESH,
        )

    @pl.loop(0, S)
    def _(step):
        grp = lax.rem(me_s + 1 + step, S)
        for sb in range(G // rb):
            rows = slice(sb * rb, sb * rb + rb)
            table = tab[grp, rows, :]
            packed = halo_recv[0, grp, rows, :].astype(F32)
            lefts = [packed, pltpu.roll(packed, 6, 1), pltpu.roll(packed, 12, 1)]
            for c in range(chunks):
                cols = slice(c * W, c * W + W)
                feats = []
                for i, stream in enumerate((q, k, v)):
                    here = stream[grp, rows, cols].astype(F32)
                    wide = jnp.concatenate([lefts[i], here], axis=1)
                    total = column(table, i, 0) * here
                    for j in range(1, 7):
                        total += column(table, i, j) * pltpu.roll(wide, j, 1)[:, LANES:]
                    lefts[i] = here[:, W - LANES :]
                    feats.append(total)
                short = feats[0].astype(BF16)
                qs[grp, rows, cols] = short
                feat1[grp, rows, cols] = feats[1]
                feat2[grp, rows, cols] = feats[2]
                x_send[grp, rows, cols] = (feats[1] * feats[2]).astype(BF16)
                g_send[grp, rows, cols] = (
                    g[grp, rows, cols].astype(F32) * short.astype(F32)
                ).astype(BF16)

        @pl.when(step < S - 1)
        def _():
            exchange(1, x_send, x_recv, grp).start()

    @pl.loop(0, S - 1)
    def _(step):
        exchange(2, g_send, g_recv, lax.rem(me_s + 1 + step, S)).start()

    own_x = pltpu.make_async_copy(x_send.at[me_s], x_recv.at[me_s], own_sem.at[1])
    own_g = pltpu.make_async_copy(g_send.at[me_s], g_recv.at[me_s], own_sem.at[2])
    own_x.start()
    own_g.start()

    def got(n, recv, count):
        pltpu.make_async_copy(recv.at[pl.ds(0, count)], recv.at[pl.ds(0, count)], rsem.at[n]).wait()

    def spectrum(recv, spec):
        sources, _, width = recv.shape
        per = width // LANES
        for blk in range(G // rb):
            rows = slice(blk * rb, blk * rb + rb)

            @pl.loop(0, sources)
            def _(s):
                for r in range(per):
                    at = pl.multiple_of((s * per + r) * rb, rb)
                    rt[pl.ds(at, rb), :] = recv[s, rows, r * LANES : (r + 1) * LANES].astype(F32)

            @pl.loop(0, rb // 2)
            def _(p):
                pair = [rt[pl.ds(2 * p + h, half, stride=rb), :] for h in range(2)]
                data = jnp.concatenate(pair, axis=1).astype(BF16)
                out = jnp.dot(first_ref[...], data, preferred_element_type=F32)
                cos, sin = twist_ref[0], twist_ref[1]
                for h in range(2):
                    re = out[:half, h * LANES : (h + 1) * LANES]
                    im = out[half:, h * LANES : (h + 1) * LANES]
                    turned = jnp.concatenate(
                        [re * cos + im * sin, im * cos - re * sin], axis=1
                    ).astype(BF16)
                    spec[blk * rb + 2 * p + h] = jnp.dot(
                        turned, cols_ref[...], preferred_element_type=F32
                    ).astype(spec.dtype)

    def convolve(spec_a, spec_b, conj, send, blk):
        targets, _, width = send.shape
        per = width // LANES
        rows = slice(blk * rb, blk * rb + rb)

        @pl.loop(0, rb // 2)
        def _(p):
            parts = []
            cos, sin = twist_back_ref[0], twist_back_ref[1]
            for h in range(2):
                a = spec_a[blk * rb + 2 * p + h].astype(F32)
                b = spec_b[blk * rb + 2 * p + h].astype(F32)
                ar, ai, br, bi = a[:, :LANES], a[:, LANES:], b[:, :LANES], b[:, LANES:]
                if conj:
                    re, im = ar * br + ai * bi, ar * bi - ai * br
                else:
                    re, im = ar * br - ai * bi, ar * bi + ai * br
                prod = jnp.concatenate([re, im], axis=1).astype(BF16)
                back = jnp.dot(prod, cols_back_ref[...], preferred_element_type=F32)
                re, im = back[:, :LANES], back[:, LANES:]
                parts.append(
                    jnp.concatenate([re * cos - im * sin, im * cos + re * sin], axis=0)
                )
            data = jnp.concatenate(parts, axis=1).astype(BF16)
            out = jnp.dot(last_ref[...], data, preferred_element_type=F32)
            for h in range(2):
                rt[pl.ds(2 * p + h, half, stride=rb), :] = out[:, h * LANES : (h + 1) * LANES]

        @pl.loop(0, targets)
        def _(s):
            for r in range(per):
                at = pl.multiple_of((s * per + r) * rb, rb)
                send[s, rows, r * LANES : (r + 1) * LANES] = rt[pl.ds(at, rb), :].astype(BF16)

    def send_back(n, send, recv, blk):
        rows = pl.ds(blk * rb, rb)

        @pl.loop(1, S)
        def _(d):
            t = lax.rem(me_s + d, S)
            pltpu.make_async_remote_copy(
                src_ref=send.at[t, rows], dst_ref=recv.at[me_s, rows],
                send_sem=ssem.at[n], recv_sem=rsem.at[n],
                device_id=(t, me_c), device_id_type=MESH,
            ).start()

    blocks = G // rb
    own_filter.wait()
    got(0, filt_recv, ndev - 1)
    spectrum(filt_recv, spec_k)
    own_x.wait()
    got(1, x_recv, S - 1)
    spectrum(x_recv, spec_x)
    for blk in range(blocks):
        convolve(spec_k, spec_x, False, y_send, blk)
        send_back(3, y_send, y_recv, blk)
    own_y = pltpu.make_async_copy(y_send.at[me_s], y_recv.at[me_s], own_sem.at[3])
    own_y.start()
    own_g.wait()
    got(2, g_recv, S - 1)
    spectrum(g_recv, spec_g)
    for blk in range(blocks):
        convolve(spec_k, spec_g, True, b_send, blk)
        send_back(4, b_send, b_recv, blk)
    own_b = pltpu.make_async_copy(b_send.at[me_s], b_recv.at[me_s], own_sem.at[4])
    own_b.start()
    for blk in range(blocks):
        convolve(spec_x, spec_g, True, f_send, blk)
        rows = pl.ds(blk * rb, rb)

        @pl.loop(1, ndev)
        def _(d):
            t = lax.rem(me + d, ndev)
            pltpu.make_async_remote_copy(
                src_ref=f_send.at[t, rows], dst_ref=gf_hbm.at[me_c * S + me_s, rows],
                send_sem=ssem.at[5], recv_sem=rsem.at[5],
                device_id=(t // H, lax.rem(t, H)), device_id_type=MESH,
            ).start()

    own_f = pltpu.make_async_copy(f_send.at[me], gf_hbm.at[me_c * S + me_s], own_sem.at[5])
    own_f.start()

    def lane_sum(value):
        return jnp.sum(value, axis=1, keepdims=True)

    def fold(value):
        total = value[:, :LANES]
        for at in range(LANES, value.shape[1], LANES):
            total = total + value[:, at : at + LANES]
        return total

    def back_short(i, feats, right, stream, dst, grp, rows, table):
        acc = [None] * 7
        for c in range(chunks):
            cols = slice(c * W, c * W + W)
            here = feats[grp, rows, cols].astype(F32)
            if c + 1 < chunks:
                after = feats[grp, rows, c * W + W : c * W + W + LANES].astype(F32)
            else:
                after = right
            wide = jnp.concatenate([here, after], axis=1)
            value = stream[grp, rows, cols].astype(F32)
            total = None
            for j in range(7):
                shifted = here if j == 0 else pltpu.roll(wide, W + LANES - j, 1)[:, :W]
                term = column(table, i, j) * shifted
                total = term if j == 0 else total + term
                piece = fold(shifted * value)
                acc[j] = piece if c == 0 else acc[j] + piece
            dst[grp, rows, cols] = total.astype(BF16)
        result = jnp.zeros((rb, LANES), F32)
        for j in range(7):
            result = jnp.where(lane == 8 * i + j, lane_sum(acc[j]), result)
        return result

    own_y.wait()
    got(3, y_recv, S - 1)

    @pl.loop(0, S)
    def _(grp):
        for sb in range(G // rb):
            rows = slice(sb * rb, sb * rb + rb)
            table = tab[grp, rows, :]
            acc = jnp.zeros((rb, LANES), F32)
            for c in range(chunks):
                cols = slice(c * W, c * W + W)
                mixer = x_send[grp, rows, cols].astype(F32)
                gate = y_recv[grp, rows, cols].astype(F32) + table[:, 7:8] * mixer
                short = qs[grp, rows, cols].astype(F32)
                grad = g[grp, rows, cols].astype(F32)
                mixed[grp, rows, cols] = (short * gate).astype(BF16)
                gf0[grp, rows, cols] = (grad * gate).astype(BF16)
                acc += fold(grad * short * mixer)
            part[grp, rows, :] = jnp.where(lane == 7, lane_sum(acc), 0.0)
            halo_send[1, grp, rows, :] = gf0[grp, rows, 0:LANES]

    @pl.when(me_s > 0)
    def _():
        halo_copy(1, -1).start()

    outs = [pltpu.make_async_copy(mixed, mixed_hbm, out_sem.at[0])]
    outs[0].start()

    @pl.when(me_s < S - 1)
    def _():
        halo_copy(1, 1).wait_recv()

    @pl.when(me_s == S - 1)
    def _():
        halo_recv[1] = jnp.zeros(halo_recv.shape[1:], BF16)

    @pl.loop(0, S)
    def _(grp):
        for sb in range(G // rb):
            rows = slice(sb * rb, sb * rb + rb)
            right = halo_recv[1, grp, rows, :].astype(F32)
            part[grp, rows, :] += back_short(
                0, gf0, right, q, gq, grp, rows, tab[grp, rows, :]
            )

    outs.append(pltpu.make_async_copy(gq, gq_hbm, out_sem.at[1]))
    outs[1].start()

    own_b.wait()
    got(4, b_recv, S - 1)

    @pl.loop(0, S)
    def _(grp):
        for sb in range(G // rb):
            rows = slice(sb * rb, sb * rb + rb)
            table = tab[grp, rows, :]
            for c in range(chunks):
                cols = slice(c * W, c * W + W)
                inner = g[grp, rows, cols].astype(F32) * qs[grp, rows, cols].astype(F32)
                grad = (b_recv[grp, rows, cols].astype(F32) + table[:, 7:8] * inner).astype(BF16)
                grad = grad.astype(F32)
                one = (grad * feat2[grp, rows, cols]).astype(BF16)
                two = (grad * feat1[grp, rows, cols]).astype(BF16)
                gf1[grp, rows, cols] = one
                gf2[grp, rows, cols] = two
                if c == 0:
                    packed = jnp.where(
                        lane < 6,
                        one[:, :LANES].astype(F32),
                        pltpu.roll(two[:, :LANES].astype(F32), 6, 1),
                    )
                    halo_send[2, grp, rows, :] = packed.astype(BF16)

    @pl.when(me_s > 0)
    def _():
        halo_copy(2, -1).start()

    @pl.when(me_s < S - 1)
    def _():
        halo_copy(2, 1).wait_recv()

    @pl.when(me_s == S - 1)
    def _():
        halo_recv[2] = jnp.zeros(halo_recv.shape[1:], BF16)

    @pl.loop(0, S)
    def _(grp):
        for sb in range(G // rb):
            rows = slice(sb * rb, sb * rb + rb)
            right = halo_recv[2, grp, rows, :].astype(F32)
            table = tab[grp, rows, :]
            one = back_short(1, gf1, right, k, gk, grp, rows, table)
            two = back_short(
                2, gf2, pltpu.roll(right, LANES - 6, 1), v, gv, grp, rows, table
            )
            part[grp, rows, :] += one + two

    outs.append(pltpu.make_async_copy(gk, gk_hbm, out_sem.at[2]))
    outs.append(pltpu.make_async_copy(gv, gv_hbm, out_sem.at[3]))
    outs[2].start()
    outs[3].start()

    sums_send[...] = jnp.transpose(part[...].reshape(S * G, LANES))[0:24, :]
    sums_recv[me_s] = sums_send[...]

    @pl.loop(1, S)
    def _(d):
        t = lax.rem(me_s + d, S)
        pltpu.make_async_remote_copy(
            src_ref=sums_send, dst_ref=sums_recv.at[me_s],
            send_sem=ssem.at[6], recv_sem=rsem.at[6],
            device_id=(t, me_c), device_id_type=MESH,
        ).start()

    got(6, sums_recv, S - 1)
    total = sums_recv[0]
    for s in range(1, S):
        total = total + sums_recv[s]
    total = total * scale_root
    for i in range(3):
        short_out[i] = total[8 * i : 8 * i + 7, :]
    skip_out[...] = total[7:8, :]

    def sent(n, send, count):
        pltpu.make_async_copy(send.at[pl.ds(0, count)], send.at[pl.ds(0, count)], ssem.at[n]).wait()

    sent(0, filt_recv, ndev - 1)
    sent(1, x_send, S - 1)
    sent(2, g_send, S - 1)
    sent(3, y_send, S - 1)
    sent(4, b_send, S - 1)
    sent(5, f_send, ndev - 1)
    sent(6, sums_recv, S - 1)

    @pl.when(me_s < S - 1)
    def _():
        halo_copy(0, 1).wait_send()

    for which in (1, 2):

        @pl.when(me_s > 0)
        def _():
            halo_copy(which, -1).wait_send()

    for copy in outs:
        copy.wait()
    own_f.wait()
    got(5, gf_hbm, ndev - 1)


def per_device(query_proj, key_proj, value_proj, short_taps, skip_gain, filter_raw, grad_out):
    channels, T = query_proj.shape
    S = lax.axis_size("seq")
    H = lax.axis_size("chan")
    G = channels // S
    FT = filter_raw.shape[1]
    half = S * T // LANES
    rb = min(16, G)
    split = lambda a: a.reshape(S, G, T)
    tables = make_tables(S * T)
    any_spec = pl.BlockSpec(memory_space=pl.ANY)
    vmem = pl.BlockSpec(memory_space=pltpu.VMEM)
    stream = jax.ShapeDtypeStruct((S, G, T), BF16)
    held = pltpu.VMEM((S, G, T), BF16)
    spec = pltpu.VMEM((G, half, 2 * LANES), F32)
    outs = pl.pallas_call(
        functools.partial(kernel, (S, H, G, T, FT)),
        out_shape=(
            stream, stream, stream, stream,
            jax.ShapeDtypeStruct((3, 7, channels), F32),
            jax.ShapeDtypeStruct((1, channels), F32),
            jax.ShapeDtypeStruct((H * S, G, FT), BF16),
        ),
        in_specs=[any_spec] * 4 + [vmem] * 2 + [any_spec] + [vmem] * 6,
        out_specs=(any_spec,) * 4 + (vmem,) * 2 + (any_spec,),
        scratch_shapes=[
            held, held, held, held,
            pltpu.VMEM((LANES, channels), F32),
            pltpu.VMEM((S, G, LANES), F32),
            pltpu.VMEM((S, G, LANES), F32),
            held,
            pltpu.VMEM((S, G, T), F32),
            pltpu.VMEM((S, G, T), F32),
            pltpu.VMEM((3, S, G, LANES), BF16),
            pltpu.VMEM((3, S, G, LANES), BF16),
            held, held,
            pltpu.VMEM((S * H, G, FT), BF16),
            held, held,
            pltpu.VMEM((half * rb, LANES), F32),
            spec, spec, spec,
            held, held,
            pltpu.VMEM((S * H, G, FT), BF16),
            held, held,
            held, held, held,
            held, held, held, held,
            pltpu.VMEM((24, channels), F32),
            pltpu.VMEM((S, 24, channels), F32),
            pltpu.SemaphoreType.DMA((4,)),
            pltpu.SemaphoreType.DMA((4,)),
            pltpu.SemaphoreType.DMA((6,)),
            pltpu.SemaphoreType.DMA((3,)),
            pltpu.SemaphoreType.DMA((3,)),
            pltpu.SemaphoreType.DMA((7,)),
            pltpu.SemaphoreType.DMA((7,)),
        ],
        compiler_params=pltpu.CompilerParams(
            collective_id=0, has_side_effects=True, vmem_limit_bytes=58 * 2**20
        ),
        cost_estimate=pl.CostEstimate(
            flops=6 * 4 * channels * T * S * 16, bytes_accessed=12 * channels * T * 2, transcendentals=0
        ),
    )(
        split(query_proj), split(key_proj), split(value_proj), split(grad_out),
        short_taps, skip_gain.reshape(1, channels), filter_raw.reshape(H * S, G, FT),
        *tables,
    )
    mixed, gq, gk, gv, short, skip, gf = outs
    back = lambda a: a.reshape(channels, T)
    return (
        back(mixed), back(gq), back(gk), back(gv), short, skip.reshape(channels),
        gf.reshape(H * S * G, FT),
    )


def solution(mesh):
    placed = (
        P("chan", "seq"),
        P("chan", "seq"),
        P("chan", "seq"),
        P(None, None, "chan"),
        P("chan"),
        P(None, ("seq", "chan")),
        P("chan", "seq"),
    )
    return jax.shard_map(
        per_device,
        mesh=mesh,
        in_specs=placed,
        out_specs=(
            P("chan", "seq"),
            P("chan", "seq"),
            P("chan", "seq"),
            P("chan", "seq"),
            P(None, None, "chan"),
            P("chan"),
            P(None, ("seq", "chan")),
        ),
        check_vma=False,
    )
```

```python
import functools
import math

import jax
import jax.numpy as jnp
import numpy as np
from jax import lax
from jax.experimental import pallas as pl
from jax.experimental.pallas import tpu as pltpu
from jax.sharding import PartitionSpec as P
import ml_dtypes

MESH = pl.DeviceIdType.MESH
F32 = jnp.float32
BF16 = jnp.bfloat16
LANES = 128


def make_tables(length):
    points = 2 * length
    rows = points // LANES
    half = rows // 2
    n1 = np.arange(half, dtype=np.float64)
    k1 = np.arange(half, dtype=np.float64) + 0.5
    n2 = np.arange(LANES, dtype=np.float64)
    angle = 2 * np.pi * np.outer(k1, n1) / rows
    first = np.concatenate([np.cos(angle), -np.sin(angle)], axis=0)
    last = np.concatenate([np.cos(angle.T), -np.sin(angle.T)], axis=1)
    angle = 2 * np.pi * np.outer(n2, n2) / LANES
    c, s = np.cos(angle), np.sin(angle)
    cols = np.block([[c, -s], [s, c]])
    cols_back = np.block([[c, s], [-s, c]])
    angle = 2 * np.pi * np.outer(k1, n2) / points
    scale = (2.0 / points) / math.sqrt(length)
    twist = np.stack([np.cos(angle), np.sin(angle)])
    as16 = lambda a: jnp.asarray(a.astype(np.float32).astype(ml_dtypes.bfloat16))
    as32 = lambda a: jnp.asarray(a.astype(np.float32))
    return as16(first), as16(last), as16(cols), as16(cols_back), as32(twist), as32(twist * scale)


def kernel(
    dims,
    q_hbm, k_hbm, v_hbm, g_hbm, taps_ref, skip_ref, filt_hbm,
    first_ref, last_ref, cols_ref, cols_back_ref, twist_ref, twist_back_ref,
    mixed_hbm, gq_hbm, gk_hbm, gv_hbm, short_out, skip_out, gf_hbm,
    q, k, v, g, tab_t, tab, part, qs, feat1, feat2,
    halo_send, halo_recv, x_send, g_send, filt_recv, x_recv, g_recv,
    rt, spec_k, spec_x, spec_g, y_send, b_send, f_send, y_recv, b_recv,
    gf0, gf1, gf2, mixed, gq, gk, gv, sums_send, sums_recv, total_send, total_recv,
    in_sem, out_sem, own_sem, halo_ssem, halo_rsem, ssem, rsem,
):
    S, H, G, T, FT = dims
    half = S * T // LANES
    rb = min(16, G)
    W = min(512, T)
    chunks = T // W
    ndev = S * H
    me_s = lax.axis_index("seq")
    me_c = lax.axis_index("chan")
    me = me_s * H + me_c
    scale_root = 1.0 / math.sqrt(S * T)

    ins = [
        pltpu.make_async_copy(src, dst, in_sem.at[i])
        for i, (src, dst) in enumerate(((q_hbm, q), (k_hbm, k), (v_hbm, v), (g_hbm, g)))
    ]
    for copy in ins:
        copy.start()
    barrier = pltpu.get_barrier_semaphore()

    @pl.loop(1, ndev)
    def _(d):
        t = lax.rem(me + d, ndev)
        pl.semaphore_signal(
            barrier, inc=1, device_id=(t // H, lax.rem(t, H)), device_id_type=MESH
        )

    tab_t[...] = jnp.zeros_like(tab_t)
    for i in range(3):
        tab_t[8 * i : 8 * i + 7, :] = taps_ref[i].astype(F32)
    tab_t[7:8, :] = skip_ref[...]
    tab[...] = jnp.transpose(tab_t[...]).reshape(tab.shape)

    lane = lax.broadcasted_iota(jnp.int32, (rb, LANES), 1)
    for copy in ins[:3]:
        copy.wait()

    def pack(which, edges):
        for hb in range(max(1, S // 8)):
            for sb in range(G // rb):
                rows = slice(sb * rb, sb * rb + rb)
                packed = jnp.zeros((rb, LANES), F32)
                for slot in range(min(8, S)):
                    for n, (ref, at, offset) in enumerate(edges):
                        block = ref[hb * 8 + slot, rows, at : at + LANES].astype(F32)
                        begin = 16 * slot + 6 * n
                        shift = (begin - offset) % LANES
                        if shift:
                            block = pltpu.roll(block, shift, 1)
                        packed = jnp.where((lane >= begin) & (lane < begin + 6), block, packed)
                halo_send[which, hb, rows, :] = packed.astype(BF16)

    def unpack(which, grp, rows, n, offset):
        packed = halo_recv[which, grp // 8, rows, :].astype(F32)
        shift = lax.rem(offset - 6 * n - 16 * lax.rem(grp, 8) + 2 * LANES, LANES)
        return pltpu.roll(packed, shift, 1)

    pack(0, ((q, T - LANES, LANES - 6), (k, T - LANES, LANES - 6)))
    pack(1, ((v, T - LANES, LANES - 6),))
    pl.semaphore_wait(barrier, ndev - 1)

    def halo_copy(which, step):
        target = lax.rem(me_s + step + S, S)
        blocks = pl.ds(0, 2) if which == 0 else pl.ds(which, 1)
        return pltpu.make_async_remote_copy(
            src_ref=halo_send.at[blocks], dst_ref=halo_recv.at[blocks],
            send_sem=halo_ssem.at[which], recv_sem=halo_rsem.at[which],
            device_id=(target, me_c), device_id_type=MESH,
        )

    @pl.when(me_s < S - 1)
    def _():
        halo_copy(0, 1).start()

    @pl.loop(1, ndev)
    def _(d):
        t = lax.rem(me + d, ndev)
        ts, tc = t // H, lax.rem(t, H)
        pltpu.make_async_remote_copy(
            src_ref=filt_hbm.at[tc * S + ts], dst_ref=filt_recv.at[me],
            send_sem=ssem.at[0], recv_sem=rsem.at[0],
            device_id=(ts, tc), device_id_type=MESH,
        ).start()

    own_filter = pltpu.make_async_copy(
        filt_hbm.at[me_c * S + me_s], filt_recv.at[me], own_sem.at[0]
    )
    own_filter.start()
    ins[3].wait()

    @pl.when(me_s > 0)
    def _():
        halo_copy(0, -1).wait_recv()

    @pl.when(me_s == 0)
    def _():
        halo_recv[0:2] = jnp.zeros((2,) + halo_recv.shape[1:], BF16)

    def column(table, i, j):
        return table[:, 8 * i + j : 8 * i + j + 1]

    def exchange(n, send, recv, grp):
        return pltpu.make_async_remote_copy(
            src_ref=send.at[grp], dst_ref=recv.at[me_s],
            send_sem=ssem.at[n], recv_sem=rsem.at[n],
            device_id=(grp, me_c), device_id_type=MESH,
        )

    @pl.loop(0, S)
    def _(step):
        grp = lax.rem(me_s + 1 + step, S)
        for sb in range(G // rb):
            rows = slice(sb * rb, sb * rb + rb)
            table = tab[grp, rows, :]
            lefts = [unpack(n // 2, grp, rows, n % 2, LANES - 6) for n in range(3)]
            for c in range(chunks):
                cols = slice(c * W, c * W + W)
                feats = []
                for i, stream in enumerate((q, k, v)):
                    here = stream[grp, rows, cols].astype(F32)
                    wide = jnp.concatenate([lefts[i], here], axis=1)
                    total = column(table, i, 0) * here
                    for j in range(1, 7):
                        total += column(table, i, j) * pltpu.roll(wide, j, 1)[:, LANES:]
                    lefts[i] = here[:, W - LANES :]
                    feats.append(total)
                short = feats[0].astype(BF16)
                qs[grp, rows, cols] = short
                feat1[grp, rows, cols] = feats[1]
                feat2[grp, rows, cols] = feats[2]
                x_send[grp, rows, cols] = (feats[1] * feats[2]).astype(BF16)
                g_send[grp, rows, cols] = (
                    g[grp, rows, cols].astype(F32) * short.astype(F32)
                ).astype(BF16)

        @pl.when(step < S - 1)
        def _():
            exchange(1, x_send, x_recv, grp).start()

    own_x = pltpu.make_async_copy(x_send.at[me_s], x_recv.at[me_s], own_sem.at[1])
    own_g = pltpu.make_async_copy(g_send.at[me_s], g_recv.at[me_s], own_sem.at[2])
    own_x.start()
    own_g.start()

    def got(n, recv, count):
        pltpu.make_async_copy(recv.at[pl.ds(0, count)], recv.at[pl.ds(0, count)], rsem.at[n]).wait()

    def spectrum(recv, spec):
        sources, _, width = recv.shape
        per = width // LANES
        for blk in range(G // rb):
            rows = slice(blk * rb, blk * rb + rb)

            @pl.loop(0, sources)
            def _(s):
                for r in range(per):
                    at = pl.multiple_of((s * per + r) * rb, rb)
                    rt[pl.ds(at, rb), :] = recv[s, rows, r * LANES : (r + 1) * LANES].astype(F32)

            @pl.loop(0, rb // 2)
            def _(p):
                pair = [rt[pl.ds(2 * p + h, half, stride=rb), :] for h in range(2)]
                data = jnp.concatenate(pair, axis=1).astype(BF16)
                out = jnp.dot(first_ref[...], data, preferred_element_type=F32)
                cos, sin = twist_ref[0], twist_ref[1]
                for h in range(2):
                    re = out[:half, h * LANES : (h + 1) * LANES]
                    im = out[half:, h * LANES : (h + 1) * LANES]
                    turned = jnp.concatenate(
                        [re * cos + im * sin, im * cos - re * sin], axis=1
                    ).astype(BF16)
                    spec[blk * rb + 2 * p + h] = jnp.dot(
                        turned, cols_ref[...], preferred_element_type=F32
                    ).astype(spec.dtype)

    def convolve(spec_a, spec_b, conj, send, blk):
        targets, _, width = send.shape
        per = width // LANES
        rows = slice(blk * rb, blk * rb + rb)

        @pl.loop(0, rb // 2)
        def _(p):
            parts = []
            cos, sin = twist_back_ref[0], twist_back_ref[1]
            for h in range(2):
                a = spec_a[blk * rb + 2 * p + h].astype(F32)
                b = spec_b[blk * rb + 2 * p + h].astype(F32)
                ar, ai, br, bi = a[:, :LANES], a[:, LANES:], b[:, :LANES], b[:, LANES:]
                if conj:
                    re, im = ar * br + ai * bi, ar * bi - ai * br
                else:
                    re, im = ar * br - ai * bi, ar * bi + ai * br
                prod = jnp.concatenate([re, im], axis=1).astype(BF16)
                back = jnp.dot(prod, cols_back_ref[...], preferred_element_type=F32)
                re, im = back[:, :LANES], back[:, LANES:]
                parts.append(
                    jnp.concatenate([re * cos - im * sin, im * cos + re * sin], axis=0)
                )
            data = jnp.concatenate(parts, axis=1).astype(BF16)
            out = jnp.dot(last_ref[...], data, preferred_element_type=F32)
            for h in range(2):
                rt[pl.ds(2 * p + h, half, stride=rb), :] = out[:, h * LANES : (h + 1) * LANES]

        @pl.loop(0, targets)
        def _(s):
            for r in range(per):
                at = pl.multiple_of((s * per + r) * rb, rb)
                send[s, rows, r * LANES : (r + 1) * LANES] = rt[pl.ds(at, rb), :].astype(BF16)

    def send_back(n, send, recv, blk):
        rows = pl.ds(blk * rb, rb)

        @pl.loop(1, S)
        def _(d):
            t = lax.rem(me_s + d, S)
            pltpu.make_async_remote_copy(
                src_ref=send.at[t, rows], dst_ref=recv.at[me_s, rows],
                send_sem=ssem.at[n], recv_sem=rsem.at[n],
                device_id=(t, me_c), device_id_type=MESH,
            ).start()

    blocks = G // rb
    own_filter.wait()
    got(0, filt_recv, ndev - 1)

    @pl.loop(0, S - 1)
    def _(step):
        exchange(2, g_send, g_recv, lax.rem(me_s + 1 + step, S)).start()

    spectrum(filt_recv, spec_k)
    own_x.wait()
    got(1, x_recv, S - 1)
    spectrum(x_recv, spec_x)
    for blk in range(blocks):
        convolve(spec_k, spec_x, False, y_send, blk)
        send_back(3, y_send, y_recv, blk)
    own_y = pltpu.make_async_copy(y_send.at[me_s], y_recv.at[me_s], own_sem.at[3])
    own_y.start()
    own_g.wait()
    got(2, g_recv, S - 1)
    spectrum(g_recv, spec_g)
    for blk in range(blocks):
        convolve(spec_k, spec_g, True, b_send, blk)
        send_back(4, b_send, b_recv, blk)
    own_b = pltpu.make_async_copy(b_send.at[me_s], b_recv.at[me_s], own_sem.at[4])
    own_b.start()
    for blk in range(blocks):
        convolve(spec_x, spec_g, True, f_send, blk)

    own_f = pltpu.make_async_copy(f_send.at[me], gf_hbm.at[me_c * S + me_s], own_sem.at[5])
    own_f.start()

    def lane_sum(value):
        return jnp.sum(value, axis=1, keepdims=True)

    def fold(value):
        total = value[:, :LANES]
        for at in range(LANES, value.shape[1], LANES):
            total = total + value[:, at : at + LANES]
        return total

    def back_short(i, feats, stream, dst, left, grp, rows, table):
        acc = [None] * 7
        for c in range(chunks):
            cols = slice(c * W, c * W + W)
            here = feats[grp, rows, cols].astype(F32)
            if c + 1 < chunks:
                after = feats[grp, rows, c * W + W : c * W + W + LANES].astype(F32)
            else:
                after = jnp.zeros((rb, LANES), F32)
            wide = jnp.concatenate([here, after], axis=1)
            value = stream[grp, rows, cols].astype(F32)
            total = None
            for j in range(7):
                shifted = here if j == 0 else pltpu.roll(wide, W + LANES - j, 1)[:, :W]
                term = column(table, i, j) * shifted
                total = term if j == 0 else total + term
                piece = fold(shifted * value)
                if c == 0 and j > 0:
                    piece += jnp.where(lane < j, here[:, :LANES] * pltpu.roll(left, j, 1), 0.0)
                acc[j] = piece if c == 0 else acc[j] + piece
            dst[grp, rows, cols] = total.astype(BF16)
        result = jnp.zeros((rb, LANES), F32)
        for j in range(7):
            result = jnp.where(lane == 8 * i + j, lane_sum(acc[j]), result)
        return result

    def last_block(i, feats, right, dst, grp, rows, table):
        here = feats[grp, rows, T - LANES : T].astype(F32)
        wide = jnp.concatenate([here, right], axis=1)
        total = column(table, i, 0) * here
        for j in range(1, 7):
            total += column(table, i, j) * pltpu.roll(wide, 2 * LANES - j, 1)[:, :LANES]
        dst[grp, rows, T - LANES : T] = total.astype(BF16)

    own_y.wait()
    got(3, y_recv, S - 1)

    @pl.loop(0, S)
    def _(grp):
        for sb in range(G // rb):
            rows = slice(sb * rb, sb * rb + rb)
            table = tab[grp, rows, :]
            acc = jnp.zeros((rb, LANES), F32)
            for c in range(chunks):
                cols = slice(c * W, c * W + W)
                mixer = x_send[grp, rows, cols].astype(F32)
                gate = y_recv[grp, rows, cols].astype(F32) + table[:, 7:8] * mixer
                short = qs[grp, rows, cols].astype(F32)
                grad = g[grp, rows, cols].astype(F32)
                mixed[grp, rows, cols] = (short * gate).astype(BF16)
                gf0[grp, rows, cols] = (grad * gate).astype(BF16)
                acc += fold(grad * short * mixer)
            part[grp, rows, :] = jnp.where(lane == 7, lane_sum(acc), 0.0)

    pack(2, ((gf0, 0, 0),))

    @pl.when(me_s > 0)
    def _():
        halo_copy(2, -1).start()

    @pl.loop(1, ndev)
    def _(d):
        t = lax.rem(me + d, ndev)
        pltpu.make_async_remote_copy(
            src_ref=f_send.at[t], dst_ref=gf_hbm.at[me_c * S + me_s],
            send_sem=ssem.at[5], recv_sem=rsem.at[5],
            device_id=(t // H, lax.rem(t, H)), device_id_type=MESH,
        ).start()

    outs = [pltpu.make_async_copy(mixed, mixed_hbm, out_sem.at[0])]
    outs[0].start()

    @pl.loop(0, S)
    def _(grp):
        for sb in range(G // rb):
            rows = slice(sb * rb, sb * rb + rb)
            left = unpack(0, grp, rows, 0, LANES - 6)
            part[grp, rows, :] += back_short(0, gf0, q, gq, left, grp, rows, tab[grp, rows, :])

    @pl.when(me_s < S - 1)
    def _():
        halo_copy(2, 1).wait_recv()

    @pl.when(me_s == S - 1)
    def _():
        halo_recv[2] = jnp.zeros(halo_recv.shape[1:], BF16)

    @pl.loop(0, S)
    def _(grp):
        for sb in range(G // rb):
            rows = slice(sb * rb, sb * rb + rb)
            last_block(0, gf0, unpack(2, grp, rows, 0, 0), gq, grp, rows, tab[grp, rows, :])

    outs.append(pltpu.make_async_copy(gq, gq_hbm, out_sem.at[1]))
    outs[1].start()

    own_b.wait()
    got(4, b_recv, S - 1)

    @pl.loop(0, S)
    def _(grp):
        for sb in range(G // rb):
            rows = slice(sb * rb, sb * rb + rb)
            table = tab[grp, rows, :]
            for c in range(chunks):
                cols = slice(c * W, c * W + W)
                inner = g[grp, rows, cols].astype(F32) * qs[grp, rows, cols].astype(F32)
                grad = (b_recv[grp, rows, cols].astype(F32) + table[:, 7:8] * inner).astype(BF16)
                grad = grad.astype(F32)
                gf1[grp, rows, cols] = (grad * feat2[grp, rows, cols]).astype(BF16)
                gf2[grp, rows, cols] = (grad * feat1[grp, rows, cols]).astype(BF16)

    pack(3, ((gf1, 0, 0), (gf2, 0, 0)))

    @pl.when(me_s > 0)
    def _():
        halo_copy(3, -1).start()

    @pl.loop(0, S)
    def _(grp):
        for sb in range(G // rb):
            rows = slice(sb * rb, sb * rb + rb)
            table = tab[grp, rows, :]
            left = [unpack(n // 2, grp, rows, n % 2, LANES - 6) for n in (1, 2)]
            one = back_short(1, gf1, k, gk, left[0], grp, rows, table)
            two = back_short(2, gf2, v, gv, left[1], grp, rows, table)
            part[grp, rows, :] += one + two

    turned = jnp.transpose(part[...].reshape(S * G, LANES))
    lane8 = lax.broadcasted_iota(jnp.int32, (8, LANES), 1)

    def moved(block, shift):
        return pltpu.roll(block, shift % LANES, 1) if shift % LANES else block

    for grp in range(S):
        base = grp * G // LANES * LANES
        tile = jnp.zeros((8, LANES), F32)
        for i in range(3):
            block = turned[8 * i : 8 * i + 8, base : base + LANES]
            tile = jnp.where(lane8 // G == i, moved(block, i * G - grp * G), tile)
        sums_send[grp] = tile
    sums_recv[me_s] = sums_send[me_s]

    def sums_copy(n, src, dst, t):
        return pltpu.make_async_remote_copy(
            src_ref=src, dst_ref=dst.at[me_s], send_sem=ssem.at[n], recv_sem=rsem.at[n],
            device_id=(t, me_c), device_id_type=MESH,
        )

    @pl.loop(1, S)
    def _(d):
        t = lax.rem(me_s + d, S)
        sums_copy(6, sums_send.at[t], sums_recv, t).start()

    @pl.when(me_s < S - 1)
    def _():
        halo_copy(3, 1).wait_recv()

    @pl.when(me_s == S - 1)
    def _():
        halo_recv[3] = jnp.zeros(halo_recv.shape[1:], BF16)

    @pl.loop(0, S)
    def _(grp):
        for sb in range(G // rb):
            rows = slice(sb * rb, sb * rb + rb)
            table = tab[grp, rows, :]
            last_block(1, gf1, unpack(3, grp, rows, 0, 0), gk, grp, rows, table)
            last_block(2, gf2, unpack(3, grp, rows, 1, 0), gv, grp, rows, table)

    outs.append(pltpu.make_async_copy(gk, gk_hbm, out_sem.at[2]))
    outs.append(pltpu.make_async_copy(gv, gv_hbm, out_sem.at[3]))
    outs[2].start()
    outs[3].start()

    got(6, sums_recv, S - 1)
    total = sums_recv[0]
    for s in range(1, S):
        total = total + sums_recv[s]
    total_send[...] = total * scale_root
    total_recv[me_s] = total_send[...]

    @pl.loop(1, S)
    def _(d):
        sums_copy(7, total_send, total_recv, lax.rem(me_s + d, S)).start()

    got(7, total_recv, S - 1)
    for base in range(0, S * G, LANES):
        for i in range(3):
            block = jnp.zeros((8, LANES), F32)
            for grp in range(base // G, min(S * G, base + LANES) // G):
                mine = lane8 // G == (grp * G - base) // G
                block = jnp.where(mine, moved(total_recv[grp], grp * G - i * G), block)
            short_out[i, :, base : base + LANES] = block[0:7]
            if i == 0:
                skip_out[:, base : base + LANES] = block[7:8]

    def sent(n, send, count):
        pltpu.make_async_copy(send.at[pl.ds(0, count)], send.at[pl.ds(0, count)], ssem.at[n]).wait()

    sent(0, filt_recv, ndev - 1)
    sent(1, x_send, S - 1)
    sent(2, g_send, S - 1)
    sent(3, y_send, S - 1)
    sent(4, b_send, S - 1)
    sent(5, f_send, ndev - 1)
    sent(6, sums_recv, S - 1)
    sent(7, total_recv, S - 1)

    @pl.when(me_s < S - 1)
    def _():
        halo_copy(0, 1).wait_send()

    for which in (2, 3):

        @pl.when(me_s > 0)
        def _():
            halo_copy(which, -1).wait_send()

    for copy in outs:
        copy.wait()
    own_f.wait()
    got(5, gf_hbm, ndev - 1)


def hand_on(arrays):
    pieces = [4 if a.size > 2**17 else 1 for a in arrays]
    count = len(arrays)

    def body(*refs):
        held, sem_in, sem_out = refs[2 * count : 3 * count], refs[-2], refs[-1]
        arriving, leaving = [], []
        for src, mid, dst, cuts in zip(refs, held, refs[count:], pieces):
            size = src.shape[0] // cuts
            for at in range(cuts):
                where = pl.ds(at * size, size)
                n = len(arriving)
                arriving.append(pltpu.make_async_copy(src.at[where], mid.at[where], sem_in.at[n]))
                leaving.append(pltpu.make_async_copy(mid.at[where], dst.at[where], sem_out.at[n]))
        for copy in arriving:
            copy.start()
        for one, two in zip(arriving, leaving):
            one.wait()
            two.start()
        for copy in leaving:
            copy.wait()

    spec = pl.BlockSpec(memory_space=pl.ANY)
    return pl.pallas_call(
        body,
        out_shape=tuple(jax.ShapeDtypeStruct(a.shape, a.dtype) for a in arrays),
        in_specs=[spec] * count,
        out_specs=(spec,) * count,
        scratch_shapes=[pltpu.VMEM(a.shape, a.dtype) for a in arrays]
        + [pltpu.SemaphoreType.DMA((sum(pieces),))] * 2,
        compiler_params=pltpu.CompilerParams(vmem_limit_bytes=58 * 2**20),
    )(*arrays)


def per_device(query_proj, key_proj, value_proj, short_taps, skip_gain, filter_raw, grad_out):
    channels, T = query_proj.shape
    S = lax.axis_size("seq")
    H = lax.axis_size("chan")
    G = channels // S
    FT = filter_raw.shape[1]
    half = S * T // LANES
    rb = min(16, G)
    split = lambda a: a.reshape(S, G, T)
    tables = make_tables(S * T)
    any_spec = pl.BlockSpec(memory_space=pl.ANY)
    vmem = pl.BlockSpec(memory_space=pltpu.VMEM)
    stream = jax.ShapeDtypeStruct((S, G, T), BF16)
    held = pltpu.VMEM((S, G, T), BF16)
    spec = pltpu.VMEM((G, half, 2 * LANES), F32)
    outs = pl.pallas_call(
        functools.partial(kernel, (S, H, G, T, FT)),
        out_shape=(
            stream, stream, stream, stream,
            jax.ShapeDtypeStruct((3, 7, channels), F32),
            jax.ShapeDtypeStruct((1, channels), F32),
            jax.ShapeDtypeStruct((H * S, G, FT), BF16),
        ),
        in_specs=[any_spec] * 4 + [vmem] * 2 + [any_spec] + [vmem] * 6,
        out_specs=(any_spec,) * 4 + (vmem,) * 2 + (any_spec,),
        scratch_shapes=[
            held, held, held, held,
            pltpu.VMEM((LANES, channels), F32),
            pltpu.VMEM((S, G, LANES), F32),
            pltpu.VMEM((S, G, LANES), F32),
            held,
            pltpu.VMEM((S, G, T), F32),
            pltpu.VMEM((S, G, T), F32),
            pltpu.VMEM((4, max(1, S // 8), G, LANES), BF16),
            pltpu.VMEM((4, max(1, S // 8), G, LANES), BF16),
            held, held,
            pltpu.VMEM((S * H, G, FT), BF16),
            held, held,
            pltpu.VMEM((half * rb, LANES), F32),
            spec, spec, spec,
            held, held,
            pltpu.VMEM((S * H, G, FT), BF16),
            held, held,
            held, held, held,
            held, held, held, held,
            pltpu.VMEM((S, 8, LANES), F32),
            pltpu.VMEM((S, 8, LANES), F32),
            pltpu.VMEM((8, LANES), F32),
            pltpu.VMEM((S, 8, LANES), F32),
            pltpu.SemaphoreType.DMA((4,)),
            pltpu.SemaphoreType.DMA((4,)),
            pltpu.SemaphoreType.DMA((6,)),
            pltpu.SemaphoreType.DMA((4,)),
            pltpu.SemaphoreType.DMA((4,)),
            pltpu.SemaphoreType.DMA((8,)),
            pltpu.SemaphoreType.DMA((8,)),
        ],
        compiler_params=pltpu.CompilerParams(
            collective_id=0, has_side_effects=True, vmem_limit_bytes=58 * 2**20
        ),
        cost_estimate=pl.CostEstimate(
            flops=6 * 4 * channels * T * S * 16, bytes_accessed=12 * channels * T * 2, transcendentals=0
        ),
    )(
        split(query_proj), split(key_proj), split(value_proj), split(grad_out),
        short_taps, skip_gain.reshape(1, channels), filter_raw.reshape(H * S, G, FT),
        *tables,
    )
    mixed, gq, gk, gv, short, skip, gf = hand_on(outs)
    back = lambda a: a.reshape(channels, T)
    return (
        back(mixed), back(gq), back(gk), back(gv), short, skip.reshape(channels),
        gf.reshape(H * S * G, FT),
    )


def solution(mesh):
    placed = (
        P("chan", "seq"),
        P("chan", "seq"),
        P("chan", "seq"),
        P(None, None, "chan"),
        P("chan"),
        P(None, ("seq", "chan")),
        P("chan", "seq"),
    )
    return jax.shard_map(
        per_device,
        mesh=mesh,
        in_specs=placed,
        out_specs=(
            P("chan", "seq"),
            P("chan", "seq"),
            P("chan", "seq"),
            P("chan", "seq"),
            P(None, None, "chan"),
            P("chan"),
            P(None, ("seq", "chan")),
        ),
        check_vma=False,
    )
```

```python
import functools
import math

import jax
import jax.numpy as jnp
import numpy as np
from jax import lax
from jax.experimental import pallas as pl
from jax.experimental.pallas import tpu as pltpu
from jax.sharding import PartitionSpec as P
import ml_dtypes

MESH = pl.DeviceIdType.MESH
F32 = jnp.float32
BF16 = jnp.bfloat16
LANES = 128
UNROLL = 2


class Plan:
    def __init__(self, seq, chan, channels, length):
        self.S, self.H, self.A = seq, chan, seq // 2
        self.rb = math.gcd(channels, 16 if channels >= 256 else 8)
        self.NU = channels // self.rb
        self.nb = self.NU * 5 // 8
        self.na = self.NU - self.nb
        spread = lambda n, m: [n // m + (i < n % m) for i in range(m)]
        if (seq, self.NU) == (8, 16):
            first, second, self.help = [1, 1, 2, 2], [3, 3, 2, 2], [4, 3, 2, 1]
        else:
            first, second = spread(self.na, self.A), spread(self.nb, self.A)
            self.help = spread(self.nb, self.A)
        self.full = first + second
        self.help = self.help + [0] * self.A
        self.full_base = [sum(self.full[:i]) for i in range(seq)]
        self.help_base = [self.na + sum(self.help[:i]) for i in range(seq)]
        self.nf, self.nh = max(self.full), max(self.help)
        self.T = length // seq
        self.FT = self.T // chan


def make_tables(length, whole):
    points = 2 * length
    rows = points // LANES
    half = rows // 2
    n1 = np.arange(half, dtype=np.float64)
    k1 = np.arange(half, dtype=np.float64) + 0.5
    n2 = np.arange(LANES, dtype=np.float64)
    angle = 2 * np.pi * np.outer(k1, n1) / rows
    first = np.concatenate([np.cos(angle), -np.sin(angle)], axis=0)
    last = np.concatenate([np.cos(angle.T), -np.sin(angle.T)], axis=1)
    angle = 2 * np.pi * np.outer(n2, n2) / LANES
    c, s = np.cos(angle), np.sin(angle)
    cols = np.block([[c, -s], [s, c]])
    cols_back = np.block([[c, s], [-s, c]])
    angle = 2 * np.pi * np.outer(k1, n2) / points
    scale = (2.0 / points) / math.sqrt(whole)
    twist = np.stack([np.cos(angle), np.sin(angle)])
    as16 = lambda a: jnp.asarray(a.astype(np.float32).astype(ml_dtypes.bfloat16))
    as32 = lambda a: jnp.asarray(a.astype(np.float32))
    return as16(first), as16(last), as16(cols), as16(cols_back), as32(twist), as32(twist * scale)


def kernel(
    plan,
    q_hbm, k_hbm, v_hbm, g_hbm, taps_ref, skip_ref, filt_hbm,
    first_ref, last_ref, twist_ref, twist_back_ref,
    first_h_ref, last_h_ref, twist_h_ref, twist_back_h_ref, cols_ref, cols_back_ref,
    mixed_hbm, gq_hbm, gk_hbm, gv_hbm, short_out, skip_out, gf_hbm, gf_more_hbm,
    q, k, v, g, tab_t, tab, part, qs, feat1, feat2,
    halo_send, halo_recv, x_send, g_send,
    kf_recv, xf_recv, gf_recv, kh_recv, xh_recv, gh_recv,
    rt, specs_f, specs_h, yf_send, bf_send, ff_send, yh_send, bh_send, fh_send,
    y_recv, b_recv, b_more,
    gf0, gf1, gf2, mixed, gq, gk, gv, sums_send, sums_recv, total_send, total_recv,
    in_sem, out_sem, own_sem, halo_ssem, halo_rsem, ssem, rsem,
):
    S, H, A, NU, rb, T, FT = plan.S, plan.H, plan.A, plan.NU, plan.rb, plan.T, plan.FT
    na, nb = plan.na, plan.nb
    G = NU * rb // S
    half = S * T // LANES
    W = min(512, T)
    chunks = T // W
    ndev = S * H
    me_s = lax.axis_index("seq")
    me_c = lax.axis_index("chan")
    me = me_s * H + me_c
    scale_root = 1.0 / math.sqrt(S * T)

    ins = [
        pltpu.make_async_copy(src, dst, in_sem.at[i])
        for i, (src, dst) in enumerate(((q_hbm, q), (k_hbm, k), (v_hbm, v), (g_hbm, g)))
    ]
    for copy in ins:
        copy.start()
    barrier = pltpu.get_barrier_semaphore()

    @pl.loop(1, ndev)
    def _(d):
        t = lax.rem(me + d, ndev)
        pl.semaphore_signal(
            barrier, inc=1, device_id=(t // H, lax.rem(t, H)), device_id_type=MESH
        )

    tab_t[...] = jnp.zeros_like(tab_t)
    for i in range(3):
        tab_t[8 * i : 8 * i + 7, :] = taps_ref[i].astype(F32)
    tab_t[7:8, :] = skip_ref[...]
    tab[...] = jnp.transpose(tab_t[...]).reshape(tab.shape)

    lane = lax.broadcasted_iota(jnp.int32, (rb, LANES), 1)
    for copy in ins[:3]:
        copy.wait()

    def pack(which, edges):
        for hb in range(NU // 8):
            packed = jnp.zeros((rb, LANES), F32)
            for slot in range(8):
                for n, (ref, at, offset) in enumerate(edges):
                    block = ref[hb * 8 + slot, :, at : at + LANES].astype(F32)
                    begin = 16 * slot + 6 * n
                    shift = (begin - offset) % LANES
                    if shift:
                        block = pltpu.roll(block, shift, 1)
                    packed = jnp.where((lane >= begin) & (lane < begin + 6), block, packed)
            halo_send[which, hb] = packed.astype(BF16)

    def unpack(which, unit, n, offset):
        packed = halo_recv[which, lax.div(unit, 8)].astype(F32)
        shift = lax.rem(offset - 6 * n - 16 * lax.rem(unit, 8) + 2 * LANES, LANES)
        return pltpu.roll(packed, shift, 1)

    pack(0, ((q, T - LANES, LANES - 6), (k, T - LANES, LANES - 6)))
    pack(1, ((v, T - LANES, LANES - 6),))
    pl.semaphore_wait(barrier, ndev - 1)

    def halo_copy(which, step):
        target = lax.rem(me_s + step + S, S)
        blocks = pl.ds(0, 2) if which == 0 else pl.ds(which, 1)
        return pltpu.make_async_remote_copy(
            src_ref=halo_send.at[blocks], dst_ref=halo_recv.at[blocks],
            send_sem=halo_ssem.at[which], recv_sem=halo_rsem.at[which],
            device_id=(target, me_c), device_id_type=MESH,
        )

    @pl.when(me_s < S - 1)
    def _():
        halo_copy(0, 1).start()

    def each(act):
        for at in range(S):

            @pl.when(me_s == at)
            def _():
                act(at)

    def pick(values):
        return sum(jnp.where(me_s == i, n, 0) for i, n in enumerate(values))

    def remote(n, m, src, dst, seq, chan):
        return pltpu.make_async_remote_copy(
            src_ref=src, dst_ref=dst, send_sem=ssem.at[n], recv_sem=rsem.at[m],
            device_id=(seq, chan), device_id_type=MESH,
        )

    def own_filter(at):
        copies = []
        for n, count, base, recv in (
            (0, plan.full[at], plan.full_base[at], kf_recv),
            (1, plan.help[at], plan.help_base[at], kh_recv),
        ):
            if count:
                copies.append(
                    pltpu.make_async_copy(
                        filt_hbm.at[pl.ds(me_c * NU + base, count)],
                        recv.at[me, pl.ds(0, count)],
                        own_sem.at[n],
                    )
                )
        return copies

    def send_filter(at):
        for d in range(1, S + 1):
            t = (at + d) % S
            for n, count, base, recv in (
                (0, plan.full[t], plan.full_base[t], kf_recv),
                (1, plan.help[t] if at < A else 0, plan.help_base[t], kh_recv),
            ):
                if count:

                    @pl.loop(1 if t == at else 0, H)
                    def _(e):
                        c = lax.rem(me_c + e, H)
                        remote(
                            n, n, filt_hbm.at[pl.ds(c * NU + base, count)],
                            recv.at[me, pl.ds(0, count)], t, c,
                        ).start()

        for copy in own_filter(at):
            copy.start()

    each(send_filter)

    ins[3].wait()

    @pl.when(me_s > 0)
    def _():
        halo_copy(0, -1).wait_recv()

    @pl.when(me_s == 0)
    def _():
        halo_recv[0:2] = jnp.zeros((2,) + halo_recv.shape[1:], BF16)

    def column(table, i, j):
        return table[:, 8 * i + j : 8 * i + j + 1]

    @pl.loop(0, NU)
    def _(unit):
        table = tab[unit]
        lefts = [unpack(n // 2, unit, n % 2, LANES - 6) for n in range(3)]
        for c in range(chunks):
            cols = slice(c * W, c * W + W)
            feats = []
            for i, stream in enumerate((q, k, v)):
                here = stream[unit, :, cols].astype(F32)
                wide = jnp.concatenate([lefts[i], here], axis=1)
                total = column(table, i, 0) * here
                for j in range(1, 7):
                    total += column(table, i, j) * pltpu.roll(wide, j, 1)[:, LANES:]
                lefts[i] = here[:, W - LANES :]
                feats.append(total)
            short = feats[0].astype(BF16)
            qs[unit, :, cols] = short
            feat1[unit, :, cols] = feats[1]
            feat2[unit, :, cols] = feats[2]
            x_send[unit, :, cols] = (feats[1] * feats[2]).astype(BF16)
            g_send[unit, :, cols] = (
                g[unit, :, cols].astype(F32) * short.astype(F32)
            ).astype(BF16)

    def send_streams(at):
        for exchange, send, whole, helped in ((2, g_send, gf_recv, gh_recv), (1, x_send, xf_recv, xh_recv)):
            for d in range(1, S + 1):
                t = (at + d) % S
                skip = exchange == 2 and at < A and t >= A
                for n, count, base, recv in (
                    (2 * exchange, 0 if skip else plan.full[t], plan.full_base[t], whole),
                    (2 * exchange + 1, plan.help[t] if at < A else 0, plan.help_base[t], helped),
                ):
                    if count and t == at:
                        for i in range(count):
                            recv[at, i] = send[base + i]
                    elif count:
                        remote(
                            n, n, send.at[pl.ds(base, count)], recv.at[at, pl.ds(0, count)], t, me_c
                        ).start()

    each(send_streams)

    whole = (specs_f, half, first_ref, last_ref, twist_ref, twist_back_ref)
    helped = (specs_h, half // 2, first_h_ref, last_h_ref, twist_h_ref, twist_back_h_ref)

    def spectrum(kind, which, recv, count):
        specs, rows, first, _, twist, _ = kind
        sources, _, _, width = recv.shape
        per = width // LANES

        @pl.loop(0, count)
        def _(unit):
            @pl.loop(0, sources)
            def _(s):
                for r in range(per):
                    at = pl.multiple_of((s * per + r) * rb, rb)
                    rt[pl.ds(at, rb), :] = recv[s, unit, :, r * LANES : (r + 1) * LANES].astype(F32)

            @pl.loop(0, rb // 2, unroll=UNROLL)
            def _(p):
                pair = [rt[pl.ds(2 * p + h, rows, stride=rb), :] for h in range(2)]
                data = jnp.concatenate(pair, axis=1).astype(BF16)
                out = jnp.dot(first[...], data, preferred_element_type=F32)
                cos, sin = twist[0], twist[1]
                for h in range(2):
                    re = out[:rows, h * LANES : (h + 1) * LANES]
                    im = out[rows:, h * LANES : (h + 1) * LANES]
                    turned = jnp.concatenate(
                        [re * cos + im * sin, im * cos - re * sin], axis=1
                    ).astype(BF16)
                    specs[which, unit * rb + 2 * p + h] = jnp.dot(
                        turned, cols_ref[...], preferred_element_type=F32
                    ).astype(BF16)

    def convolve(kind, first_spec, second_spec, conj, send, unit):
        specs, rows, _, last, _, twist = kind
        targets, _, _, width = send.shape
        per = width // LANES

        @pl.loop(0, rb // 2, unroll=UNROLL)
        def _(p):
            parts = []
            cos, sin = twist[0], twist[1]
            for h in range(2):
                a = specs[first_spec, unit * rb + 2 * p + h].astype(F32)
                b = specs[second_spec, unit * rb + 2 * p + h].astype(F32)
                ar, ai, br, bi = a[:, :LANES], a[:, LANES:], b[:, :LANES], b[:, LANES:]
                if conj:
                    re, im = ar * br + ai * bi, ar * bi - ai * br
                else:
                    re, im = ar * br - ai * bi, ar * bi + ai * br
                prod = jnp.concatenate([re, im], axis=1).astype(BF16)
                back = jnp.dot(prod, cols_back_ref[...], preferred_element_type=F32)
                re, im = back[:, :LANES], back[:, LANES:]
                parts.append(
                    jnp.concatenate([re * cos - im * sin, im * cos + re * sin], axis=0)
                )
            data = jnp.concatenate(parts, axis=1).astype(BF16)
            out = jnp.dot(last[...], data, preferred_element_type=F32)
            for h in range(2):
                rt[pl.ds(2 * p + h, rows, stride=rb), :] = out[:, h * LANES : (h + 1) * LANES]

        @pl.loop(0, targets)
        def _(s):
            for r in range(per):
                at = pl.multiple_of((s * per + r) * rb, rb)
                send[s, unit, :, r * LANES : (r + 1) * LANES] = rt[pl.ds(at, rb), :].astype(BF16)

    def take(n, ref, *counts):
        where = tuple(pl.ds(0, count) for count in counts)
        if min(counts) > 0:
            pltpu.make_async_copy(ref.at[where], ref.at[where], rsem.at[n]).wait()

    def sent(n, ref, *counts):
        where = tuple(pl.ds(0, count) for count in counts)
        if min(counts) > 0:
            pltpu.make_async_copy(ref.at[where], ref.at[where], ssem.at[n]).wait()

    n_full, n_help = pick(plan.full), pick(plan.help)
    full_base, help_base = pick(plan.full_base), pick(plan.help_base)

    def give_whole(n, send, recv, unit, within):
        place = full_base + unit

        @pl.loop(1, A if within else S)
        def _(d):
            t = A + lax.rem(me_s - A + d, A) if within else lax.rem(me_s + d, S)
            remote(2 * n, 2 * n, send.at[t, unit], recv.at[place], t, me_c).start()

    def give_helped(n, m, send, recv, unit):
        place = help_base + unit

        @pl.loop(1, A)
        def _(d):
            t = lax.rem(me_s + d, A)
            remote(2 * n + 1, m, send.at[t, unit], recv.at[place], t, me_c).start()

        recv[place] = send[me_s, unit]

    @pl.when(me_s >= A)
    def _():
        for s in range(A):
            gf_recv[s] = jnp.zeros(gf_recv.shape[1:], BF16)

        @pl.loop(na, NU)
        def _(unit):
            b_more[unit] = jnp.zeros(b_more.shape[1:], BF16)

    @pl.loop(0, na)
    def _(unit):
        b_more[unit] = jnp.zeros(b_more.shape[1:], BF16)

    def have_filter(at):
        for copy in own_filter(at):
            copy.wait()
        take(0, kf_recv, S * H - 1, plan.full[at])
        take(1, kh_recv, A * H - 1, plan.help[at])

    each(have_filter)
    spectrum(whole, 0, kf_recv, n_full)
    spectrum(helped, 0, kh_recv, n_help)

    def have_grad(at):
        take(4, gf_recv, (S if at < A else A) - 1, plan.full[at])
        take(5, gh_recv, A - 1, plan.help[at])

    each(have_grad)
    spectrum(whole, 2, gf_recv, n_full)
    spectrum(helped, 2, gh_recv, n_help)

    @pl.loop(0, n_full)
    def _(unit):
        convolve(whole, 0, 2, True, bf_send, unit)
        give_whole(4, bf_send, b_recv, unit, False)
        b_recv[full_base + unit] = bf_send[me_s, unit]

    @pl.loop(0, n_help)
    def _(unit):
        convolve(helped, 0, 2, True, bh_send, unit)
        give_helped(4, 9, bh_send, b_more, unit)

    def have_mixer(at):
        take(2, xf_recv, S - 1, plan.full[at])
        take(3, xh_recv, A - 1, plan.help[at])

    each(have_mixer)
    spectrum(whole, 1, xf_recv, n_full)
    spectrum(helped, 1, xh_recv, n_help)

    @pl.loop(0, n_full)
    def _(unit):
        convolve(whole, 0, 1, False, yf_send, unit)

        @pl.when(me_s < A)
        def _():
            give_whole(3, yf_send, y_recv, unit, False)

        @pl.when(me_s >= A)
        def _():
            give_whole(3, yf_send, y_recv, unit, True)

        y_recv[full_base + unit] = yf_send[me_s, unit]

    @pl.loop(0, n_help)
    def _(unit):
        convolve(helped, 0, 1, False, yh_send, unit)
        give_helped(3, 6, yh_send, y_recv, unit)

    @pl.loop(0, n_full)
    def _(unit):
        convolve(whole, 1, 2, True, ff_send, unit)

    @pl.loop(0, n_help)
    def _(unit):
        convolve(helped, 1, 2, True, fh_send, unit)

    def own_result(at):
        copies = []
        for n, count, send, dst, place in (
            (2, plan.full[at], ff_send, gf_hbm, me_c * NU + plan.full_base[at]),
            (3, plan.help[at], fh_send, gf_more_hbm, me_c * nb + plan.help_base[at] - na),
        ):
            if count:
                copies.append(
                    pltpu.make_async_copy(
                        send.at[me, pl.ds(0, count)], dst.at[pl.ds(place, count)], own_sem.at[n]
                    )
                )
        return copies

    def send_result(at):
        for n, count, send, dst, place, span in (
            (10, plan.full[at], ff_send, gf_hbm, me_c * NU + plan.full_base[at], S * H),
            (11, plan.help[at], fh_send, gf_more_hbm, me_c * nb + plan.help_base[at] - na, A * H),
        ):
            if count:

                @pl.loop(1, span)
                def _(d):
                    t = lax.rem(me + d, span)
                    remote(
                        n, n, send.at[t, pl.ds(0, count)], dst.at[pl.ds(place, count)],
                        lax.div(t, H), lax.rem(t, H),
                    ).start()

        for copy in own_result(at):
            copy.start()

    each(send_result)

    def lane_sum(value):
        return jnp.sum(value, axis=1, keepdims=True)

    def fold(value):
        total = value[:, :LANES]
        for at in range(LANES, value.shape[1], LANES):
            total = total + value[:, at : at + LANES]
        return total

    def back_short(i, feats, stream, dst, left, unit, table):
        acc = [None] * 7
        for c in range(chunks):
            cols = slice(c * W, c * W + W)
            here = feats[unit, :, cols].astype(F32)
            if c + 1 < chunks:
                after = feats[unit, :, c * W + W : c * W + W + LANES].astype(F32)
            else:
                after = jnp.zeros((rb, LANES), F32)
            wide = jnp.concatenate([here, after], axis=1)
            value = stream[unit, :, cols].astype(F32)
            total = None
            for j in range(7):
                shifted = here if j == 0 else pltpu.roll(wide, W + LANES - j, 1)[:, :W]
                term = column(table, i, j) * shifted
                total = term if j == 0 else total + term
                piece = fold(shifted * value)
                if c == 0 and j > 0:
                    piece += jnp.where(lane < j, here[:, :LANES] * pltpu.roll(left, j, 1), 0.0)
                acc[j] = piece if c == 0 else acc[j] + piece
            dst[unit, :, cols] = total.astype(BF16)
        result = jnp.zeros((rb, LANES), F32)
        for j in range(7):
            result = jnp.where(lane == 8 * i + j, lane_sum(acc[j]), result)
        return result

    def last_block(i, feats, right, dst, unit, table):
        here = feats[unit, :, T - LANES : T].astype(F32)
        wide = jnp.concatenate([here, right], axis=1)
        total = column(table, i, 0) * here
        for j in range(1, 7):
            total += column(table, i, j) * pltpu.roll(wide, 2 * LANES - j, 1)[:, :LANES]
        dst[unit, :, T - LANES : T] = total.astype(BF16)

    def have_back(at):
        take(8, b_recv, NU - plan.full[at])
        if at < A:
            take(9, b_more, nb - plan.help[at])

    each(have_back)

    @pl.loop(0, NU)
    def _(unit):
        table = tab[unit]
        for c in range(chunks):
            cols = slice(c * W, c * W + W)
            inner = g[unit, :, cols].astype(F32) * qs[unit, :, cols].astype(F32)
            back = b_recv[unit, :, cols].astype(F32) + b_more[unit, :, cols].astype(F32)
            grad = (back + table[:, 7:8] * inner).astype(BF16).astype(F32)
            gf1[unit, :, cols] = (grad * feat2[unit, :, cols]).astype(BF16)
            gf2[unit, :, cols] = (grad * feat1[unit, :, cols]).astype(BF16)

    pack(3, ((gf1, 0, 0), (gf2, 0, 0)))

    @pl.when(me_s > 0)
    def _():
        halo_copy(3, -1).start()

    @pl.loop(0, NU)
    def _(unit):
        table = tab[unit]
        left = [unpack(n // 2, unit, n % 2, LANES - 6) for n in (1, 2)]
        one = back_short(1, gf1, k, gk, left[0], unit, table)
        two = back_short(2, gf2, v, gv, left[1], unit, table)
        part[unit] = one + two

    def have_long(at):
        take(6, y_recv, NU - plan.full[at] - plan.help[at])

    each(have_long)

    @pl.loop(0, NU)
    def _(unit):
        table = tab[unit]
        acc = jnp.zeros((rb, LANES), F32)
        for c in range(chunks):
            cols = slice(c * W, c * W + W)
            mixer = x_send[unit, :, cols].astype(F32)
            gate = y_recv[unit, :, cols].astype(F32) + table[:, 7:8] * mixer
            short = qs[unit, :, cols].astype(F32)
            grad = g[unit, :, cols].astype(F32)
            mixed[unit, :, cols] = (short * gate).astype(BF16)
            gf0[unit, :, cols] = (grad * gate).astype(BF16)
            acc += fold(grad * short * mixer)
        part[unit] += jnp.where(lane == 7, lane_sum(acc), 0.0)

    pack(2, ((gf0, 0, 0),))

    @pl.when(me_s > 0)
    def _():
        halo_copy(2, -1).start()

    outs = [pltpu.make_async_copy(mixed, mixed_hbm, out_sem.at[0])]
    outs[0].start()

    @pl.loop(0, NU)
    def _(unit):
        left = unpack(0, unit, 0, LANES - 6)
        part[unit] += back_short(0, gf0, q, gq, left, unit, tab[unit])

    turned = jnp.transpose(part[...].reshape(NU * rb, LANES))
    lane8 = lax.broadcasted_iota(jnp.int32, (8, LANES), 1)

    def moved(block, shift):
        return pltpu.roll(block, shift % LANES, 1) if shift % LANES else block

    for grp in range(S):
        base = grp * G // LANES * LANES
        tile = jnp.zeros((8, LANES), F32)
        for i in range(3):
            block = turned[8 * i : 8 * i + 8, base : base + LANES]
            tile = jnp.where(lane8 // G == i, moved(block, i * G - grp * G), tile)
        sums_send[grp] = tile
    sums_recv[me_s] = sums_send[me_s]

    def sums_copy(n, src, dst, t):
        return pltpu.make_async_remote_copy(
            src_ref=src, dst_ref=dst.at[me_s], send_sem=ssem.at[n], recv_sem=rsem.at[n],
            device_id=(t, me_c), device_id_type=MESH,
        )

    @pl.loop(1, S)
    def _(d):
        t = lax.rem(me_s + d, S)
        sums_copy(12, sums_send.at[t], sums_recv, t).start()

    for which in (2, 3):

        @pl.when(me_s < S - 1)
        def _():
            halo_copy(which, 1).wait_recv()

        @pl.when(me_s == S - 1)
        def _():
            halo_recv[which] = jnp.zeros(halo_recv.shape[1:], BF16)

    @pl.loop(0, NU)
    def _(unit):
        table = tab[unit]
        last_block(0, gf0, unpack(2, unit, 0, 0), gq, unit, table)
        last_block(1, gf1, unpack(3, unit, 0, 0), gk, unit, table)
        last_block(2, gf2, unpack(3, unit, 1, 0), gv, unit, table)

    for n, (src, dst) in enumerate(((gq, gq_hbm), (gk, gk_hbm), (gv, gv_hbm))):
        outs.append(pltpu.make_async_copy(src, dst, out_sem.at[n + 1]))
        outs[-1].start()

    take(12, sums_recv, S - 1)
    total = sums_recv[0]
    for s in range(1, S):
        total = total + sums_recv[s]
    total_send[...] = total * scale_root
    total_recv[me_s] = total_send[...]

    @pl.loop(1, S)
    def _(d):
        sums_copy(13, total_send, total_recv, lax.rem(me_s + d, S)).start()

    take(13, total_recv, S - 1)
    for base in range(0, S * G, LANES):
        for i in range(3):
            block = jnp.zeros((8, LANES), F32)
            for grp in range(base // G, min(S * G, base + LANES) // G):
                mine = lane8 // G == (grp * G - base) // G
                block = jnp.where(mine, moved(total_recv[grp], grp * G - i * G), block)
            short_out[i, :, base : base + LANES] = block[0:7]
            if i == 0:
                skip_out[:, base : base + LANES] = block[7:8]

    def all_sent(at):
        full, helps = plan.full[at], plan.help[at]
        early = at < A
        sent(0, filt_hbm, NU * H - full)
        sent(2, x_send, NU - full)
        sent(4, g_send, (na if early else NU) - full)
        sent(6, yf_send, (S if early else A) - 1, full)
        sent(8, bf_send, S - 1, full)
        sent(10, ff_send, S * H - 1, full)
        if early:
            sent(1, filt_hbm, nb * H - helps)
            sent(3, x_send, nb - helps)
            sent(5, g_send, nb - helps)
            sent(7, yh_send, A - 1, helps)
            sent(9, bh_send, A - 1, helps)
            sent(11, fh_send, A * H - 1, helps)
        for copy in own_result(at):
            copy.wait()
        take(10, gf_hbm, H * NU - full)
        if early:
            take(11, gf_more_hbm, H * nb - helps)

    sent(12, sums_recv, S - 1)
    sent(13, total_recv, S - 1)

    @pl.when(me_s < S - 1)
    def _():
        halo_copy(0, 1).wait_send()

    for which in (2, 3):

        @pl.when(me_s > 0)
        def _():
            halo_copy(which, -1).wait_send()

    for copy in outs:
        copy.wait()
    each(all_sent)


def hand_on(plan, arrays, more):
    pieces = [4 if a.size > 2**17 else 1 for a in arrays]
    count = len(arrays)
    parts = [a.shape[0] // cuts for a, cuts in zip(arrays, pieces)]
    H, NU, na, nb = plan.H, plan.NU, plan.na, plan.nb

    def body(*refs):
        sources, more_ref, dests = refs[:count], refs[count], refs[count + 1 : 2 * count + 1]
        held = refs[2 * count + 1 : 3 * count + 1]
        more_held, sem_in, sem_out, sem_more = refs[3 * count + 1 :]
        arriving, leaving = [], []
        order = [count - 1] + list(range(count - 1))
        for i in order:
            for at in range(pieces[i]):
                where = pl.ds(at * parts[i], parts[i])
                n = len(arriving)
                arriving.append(
                    pltpu.make_async_copy(sources[i].at[where], held[i].at[where], sem_in.at[n])
                )
                leaving.append(
                    pltpu.make_async_copy(held[i].at[where], dests[i].at[where], sem_out.at[n])
                )
        first_half = lax.axis_index("seq") < plan.A
        extra = pltpu.make_async_copy(more_ref, more_held, sem_more)

        @pl.when(first_half)
        def _():
            extra.start()

        for copy in arriving:
            copy.start()
        last = pieces[-1]
        for one, two in zip(arriving[last:], leaving[last:]):
            one.wait()
            two.start()
        for one in arriving[:last]:
            one.wait()

        @pl.when(first_half)
        def _():
            extra.wait()
            for c in range(H):

                @pl.loop(0, nb)
                def _(i):
                    total = held[-1][c * NU + na + i].astype(F32) + more_held[c * nb + i].astype(F32)
                    held[-1][c * NU + na + i] = total.astype(BF16)

        for two in leaving[:last]:
            two.start()
        for copy in leaving:
            copy.wait()

    spec = pl.BlockSpec(memory_space=pl.ANY)
    return pl.pallas_call(
        body,
        out_shape=tuple(jax.ShapeDtypeStruct(a.shape, a.dtype) for a in arrays),
        in_specs=[spec] * (count + 1),
        out_specs=(spec,) * count,
        scratch_shapes=[pltpu.VMEM(a.shape, a.dtype) for a in arrays + (more,)]
        + [pltpu.SemaphoreType.DMA((sum(pieces),))] * 2
        + [pltpu.SemaphoreType.DMA],
        compiler_params=pltpu.CompilerParams(vmem_limit_bytes=58 * 2**20),
    )(*arrays, more)


def per_device(query_proj, key_proj, value_proj, short_taps, skip_gain, filter_raw, grad_out):
    channels, T = query_proj.shape
    S = lax.axis_size("seq")
    H = lax.axis_size("chan")
    plan = Plan(S, H, channels, S * T)
    A, NU, rb, FT, nf, nh, nb = plan.A, plan.NU, plan.rb, plan.FT, plan.nf, plan.nh, plan.nb
    half = S * T // LANES
    split = lambda a: a.reshape(NU, rb, T)
    first, last, cols, cols_back, twist, twist_back = make_tables(S * T, S * T)
    first_h, last_h, _, _, twist_h, twist_back_h = make_tables(A * T, S * T)
    any_spec = pl.BlockSpec(memory_space=pl.ANY)
    vmem = pl.BlockSpec(memory_space=pltpu.VMEM)
    stream = jax.ShapeDtypeStruct((NU, rb, T), BF16)
    held = pltpu.VMEM((NU, rb, T), BF16)
    wide = pltpu.VMEM((NU, rb, T), F32)
    edge = pltpu.VMEM((4, NU // 8, rb, LANES), BF16)
    small = pltpu.VMEM((NU, rb, LANES), F32)
    outs = pl.pallas_call(
        functools.partial(kernel, plan),
        out_shape=(
            stream, stream, stream, stream,
            jax.ShapeDtypeStruct((3, 7, channels), F32),
            jax.ShapeDtypeStruct((1, channels), F32),
            jax.ShapeDtypeStruct((H * NU, rb, FT), BF16),
            jax.ShapeDtypeStruct((H * nb, rb, FT), BF16),
        ),
        in_specs=[any_spec] * 4 + [vmem] * 2 + [any_spec] + [vmem] * 10,
        out_specs=(any_spec,) * 4 + (vmem,) * 2 + (any_spec,) * 2,
        scratch_shapes=[
            held, held, held, held,
            pltpu.VMEM((LANES, channels), F32),
            small, small,
            held, wide, wide,
            edge, edge,
            held, held,
            pltpu.VMEM((S * H, nf, rb, FT), BF16),
            pltpu.VMEM((S, nf, rb, T), BF16),
            pltpu.VMEM((S, nf, rb, T), BF16),
            pltpu.VMEM((A * H, nh, rb, FT), BF16),
            pltpu.VMEM((A, nh, rb, T), BF16),
            pltpu.VMEM((A, nh, rb, T), BF16),
            pltpu.VMEM((half * rb, LANES), F32),
            pltpu.VMEM((3, nf * rb, half, 2 * LANES), BF16),
            pltpu.VMEM((3, nh * rb, half // 2, 2 * LANES), BF16),
            pltpu.VMEM((S, nf, rb, T), BF16),
            pltpu.VMEM((S, nf, rb, T), BF16),
            pltpu.VMEM((S * H, nf, rb, FT), BF16),
            pltpu.VMEM((A, nh, rb, T), BF16),
            pltpu.VMEM((A, nh, rb, T), BF16),
            pltpu.VMEM((A * H, nh, rb, FT), BF16),
            held, held, held,
            held, held, held,
            held, held, held, held,
            pltpu.VMEM((S, 8, LANES), F32),
            pltpu.VMEM((S, 8, LANES), F32),
            pltpu.VMEM((8, LANES), F32),
            pltpu.VMEM((S, 8, LANES), F32),
            pltpu.SemaphoreType.DMA((4,)),
            pltpu.SemaphoreType.DMA((4,)),
            pltpu.SemaphoreType.DMA((4,)),
            pltpu.SemaphoreType.DMA((4,)),
            pltpu.SemaphoreType.DMA((4,)),
            pltpu.SemaphoreType.DMA((14,)),
            pltpu.SemaphoreType.DMA((14,)),
        ],
        compiler_params=pltpu.CompilerParams(
            collective_id=0, has_side_effects=True, vmem_limit_bytes=60 * 2**20
        ),
        cost_estimate=pl.CostEstimate(
            flops=6 * 4 * channels * T * S * 16, bytes_accessed=12 * channels * T * 2, transcendentals=0
        ),
    )(
        split(query_proj), split(key_proj), split(value_proj), split(grad_out),
        short_taps, skip_gain.reshape(1, channels), filter_raw.reshape(H * NU, rb, FT),
        first, last, twist, twist_back, first_h, last_h, twist_h, twist_back_h, cols, cols_back,
    )
    mixed, gq, gk, gv, short, skip, gf = hand_on(plan, outs[:-1], outs[-1])
    back = lambda a: a.reshape(channels, T)
    return (
        back(mixed), back(gq), back(gk), back(gv), short, skip.reshape(channels),
        gf.reshape(H * NU * rb, FT),
    )


def solution(mesh):
    placed = (
        P("chan", "seq"),
        P("chan", "seq"),
        P("chan", "seq"),
        P(None, None, "chan"),
        P("chan"),
        P(None, ("seq", "chan")),
        P("chan", "seq"),
    )
    return jax.shard_map(
        per_device,
        mesh=mesh,
        in_specs=placed,
        out_specs=(
            P("chan", "seq"),
            P("chan", "seq"),
            P("chan", "seq"),
            P("chan", "seq"),
            P(None, None, "chan"),
            P("chan"),
            P(None, ("seq", "chan")),
        ),
        check_vma=False,
    )
```

```python
import functools
import math

import jax
import jax.numpy as jnp
import numpy as np
from jax import lax
from jax.experimental import pallas as pl
from jax.experimental.pallas import tpu as pltpu
from jax.sharding import PartitionSpec as P
import ml_dtypes

MESH = pl.DeviceIdType.MESH
F32 = jnp.float32
BF16 = jnp.bfloat16
LANES = 128
UNROLL = 2
WAVES = (-4, -2)


class Plan:
    def __init__(self, seq, chan, channels, length):
        self.S, self.H, self.A = seq, chan, seq // 2
        self.rb = math.gcd(channels, 16 if channels >= 256 else 8)
        self.NU = channels // self.rb
        self.nb = self.NU * 5 // 8
        self.na = self.NU - self.nb
        spread = lambda n, m: [n // m + (i < n % m) for i in range(m)]
        if (seq, self.NU) == (8, 16):
            first, second, self.help = [1, 1, 2, 2], [3, 2, 3, 2], [3, 3, 2, 2]
        else:
            first, second = spread(self.na, self.A), spread(self.nb, self.A)
            self.help = spread(self.nb, self.A)
        self.full = first + second
        self.help = self.help + [0] * self.A
        self.full_base = [sum(self.full[:i]) for i in range(seq)]
        self.help_base = [self.na + sum(self.help[:i]) for i in range(seq)]
        self.nf, self.nh = max(self.full), max(self.help)
        self.T = length // seq
        self.FT = self.T // chan


def make_tables(length, whole):
    points = 2 * length
    rows = points // LANES
    half = rows // 2
    n1 = np.arange(half, dtype=np.float64)
    k1 = np.arange(half, dtype=np.float64) + 0.5
    n2 = np.arange(LANES, dtype=np.float64)
    angle = 2 * np.pi * np.outer(k1, n1) / rows
    first = np.concatenate([np.cos(angle), -np.sin(angle)], axis=0)
    last = np.concatenate([np.cos(angle.T), -np.sin(angle.T)], axis=1)
    angle = 2 * np.pi * np.outer(n2, n2) / LANES
    c, s = np.cos(angle), np.sin(angle)
    cols = np.block([[c, -s], [s, c]])
    cols_back = np.block([[c, s], [-s, c]])
    angle = 2 * np.pi * np.outer(k1, n2) / points
    scale = (2.0 / points) / math.sqrt(whole)
    twist = np.stack([np.cos(angle), np.sin(angle)])
    as16 = lambda a: jnp.asarray(a.astype(np.float32).astype(ml_dtypes.bfloat16))
    as32 = lambda a: jnp.asarray(a.astype(np.float32))
    return as16(first), as16(last), as16(cols), as16(cols_back), as32(twist), as32(twist * scale)


def kernel(
    plan,
    q_hbm, k_hbm, v_hbm, g_hbm, taps_ref, skip_ref, filt_hbm,
    tables_hbm,
    mixed_hbm, gq_hbm, gk_hbm, gv_hbm, short_out, skip_out, gf_hbm, gf_more_hbm,
    tables, q, k, v, g, tab_t, tab, part, qs, feat1, feat2,
    halo_send, halo_recv, x_send, g_send,
    kf_recv, xf_recv, gf_recv, kh_recv, xh_recv, gh_recv,
    rt, specs_f, specs_h, yf_send, bf_send, ff_send, yh_send, bh_send, fh_send,
    y_recv, b_recv, b_more,
    gf0, gf1, gf2, mixed, gq, gk, gv, sums_send, sums_recv, total_send, total_recv,
    table_sem, in_sem, out_sem, own_sem, halo_ssem, halo_rsem, ssem, rsem,
):
    S, H, A, NU, rb, T, FT = plan.S, plan.H, plan.A, plan.NU, plan.rb, plan.T, plan.FT
    na, nb = plan.na, plan.nb
    G = NU * rb // S
    half = S * T // LANES
    W = min(512, T)
    chunks = T // W
    ndev = S * H
    me_s = lax.axis_index("seq")
    me_c = lax.axis_index("chan")
    me = me_s * H + me_c
    scale_root = 1.0 / math.sqrt(S * T)

    (
        first_ref, last_ref, twist_ref, twist_back_ref,
        first_h_ref, last_h_ref, twist_h_ref, twist_back_h_ref, cols_ref, cols_back_ref,
    ) = tables
    table_copies = [
        pltpu.make_async_copy(src, dst, table_sem.at[i])
        for i, (src, dst) in enumerate(zip(tables_hbm, tables))
    ]

    ins = [
        pltpu.make_async_copy(src, dst, in_sem.at[i])
        for i, (src, dst) in enumerate(((q_hbm, q), (k_hbm, k), (v_hbm, v), (g_hbm, g)))
    ]
    for copy in ins:
        copy.start()
    barrier = pltpu.get_barrier_semaphore()

    @pl.loop(1, ndev)
    def _(d):
        t = lax.rem(me + d, ndev)
        pl.semaphore_signal(
            barrier, inc=1, device_id=(t // H, lax.rem(t, H)), device_id_type=MESH
        )

    tab_t[...] = jnp.zeros_like(tab_t)
    for i in range(3):
        tab_t[8 * i : 8 * i + 7, :] = taps_ref[i].astype(F32)
    tab_t[7:8, :] = skip_ref[...]
    tab[...] = jnp.transpose(tab_t[...]).reshape(tab.shape)

    lane = lax.broadcasted_iota(jnp.int32, (rb, LANES), 1)
    for copy in ins[:3]:
        copy.wait()

    def pack(which, edges):
        for hb in range(NU // 8):
            packed = jnp.zeros((rb, LANES), F32)
            for slot in range(8):
                for n, (ref, at, offset) in enumerate(edges):
                    block = ref[hb * 8 + slot, :, at : at + LANES].astype(F32)
                    begin = 16 * slot + 6 * n
                    shift = (begin - offset) % LANES
                    if shift:
                        block = pltpu.roll(block, shift, 1)
                    packed = jnp.where((lane >= begin) & (lane < begin + 6), block, packed)
            halo_send[which, hb] = packed.astype(BF16)

    def unpack(which, unit, n, offset):
        packed = halo_recv[which, lax.div(unit, 8)].astype(F32)
        shift = lax.rem(offset - 6 * n - 16 * lax.rem(unit, 8) + 2 * LANES, LANES)
        return pltpu.roll(packed, shift, 1)

    pack(0, ((q, T - LANES, LANES - 6), (k, T - LANES, LANES - 6)))
    pack(1, ((v, T - LANES, LANES - 6),))
    pl.semaphore_wait(barrier, ndev - 1)

    def halo_copy(which, step):
        target = lax.rem(me_s + step + S, S)
        blocks = pl.ds(0, 2) if which == 0 else pl.ds(which, 1)
        return pltpu.make_async_remote_copy(
            src_ref=halo_send.at[blocks], dst_ref=halo_recv.at[blocks],
            send_sem=halo_ssem.at[which], recv_sem=halo_rsem.at[which],
            device_id=(target, me_c), device_id_type=MESH,
        )

    @pl.when(me_s < S - 1)
    def _():
        halo_copy(0, 1).start()

    def partner(at, j):
        d = (j + 1) % S
        return ((at // A + 1 + d % 2) % 2) * A + (at % A + d // 2) % A

    def partner_here(j):
        d = lax.rem(j + 1, S)
        side = lax.rem(lax.div(me_s, A) + 1 + lax.rem(d, 2), 2)
        return side * A + lax.rem(lax.rem(me_s, A) + lax.div(d, 2), A)

    def each(act):
        for at in range(S):

            @pl.when(me_s == at)
            def _():
                act(at)

    def pick(values):
        return sum(jnp.where(me_s == i, n, 0) for i, n in enumerate(values))

    def remote(n, m, src, dst, seq, chan):
        return pltpu.make_async_remote_copy(
            src_ref=src, dst_ref=dst, send_sem=ssem.at[n], recv_sem=rsem.at[m],
            device_id=(seq, chan), device_id_type=MESH,
        )

    def own_filter(at):
        copies = []
        for n, count, base, recv in (
            (0, plan.full[at], plan.full_base[at], kf_recv),
            (1, plan.help[at], plan.help_base[at], kh_recv),
        ):
            if count:
                copies.append(
                    pltpu.make_async_copy(
                        filt_hbm.at[pl.ds(me_c * NU + base, count)],
                        recv.at[me, pl.ds(0, count)],
                        own_sem.at[n],
                    )
                )
        return copies

    def send_filter(at):
        for j in range(1, S + 1):
            t = partner(at, j)
            for n, count, base, recv in (
                (0, plan.full[t], plan.full_base[t], kf_recv),
                (1, plan.help[t] if at < A else 0, plan.help_base[t], kh_recv),
            ):
                if count:

                    @pl.loop(1 if t == at else 0, H)
                    def _(e):
                        c = lax.rem(me_c + e, H)
                        remote(
                            n, n, filt_hbm.at[pl.ds(c * NU + base, count)],
                            recv.at[me, pl.ds(0, count)], t, c,
                        ).start()

        for copy in own_filter(at):
            copy.start()

    each(send_filter)
    for copy in table_copies:
        copy.start()


    ins[3].wait()

    @pl.when(me_s > 0)
    def _():
        halo_copy(0, -1).wait_recv()

    @pl.when(me_s == 0)
    def _():
        halo_recv[0:2] = jnp.zeros((2,) + halo_recv.shape[1:], BF16)

    def column(table, i, j):
        return table[:, 8 * i + j : 8 * i + j + 1]

    @pl.loop(0, NU)
    def _(unit):
        table = tab[unit]
        lefts = [unpack(n // 2, unit, n % 2, LANES - 6) for n in range(3)]
        for c in range(chunks):
            cols = slice(c * W, c * W + W)
            feats = []
            for i, stream in enumerate((q, k, v)):
                here = stream[unit, :, cols].astype(F32)
                wide = jnp.concatenate([lefts[i], here], axis=1)
                total = column(table, i, 0) * here
                for j in range(1, 7):
                    total += column(table, i, j) * pltpu.roll(wide, j, 1)[:, LANES:]
                lefts[i] = here[:, W - LANES :]
                feats.append(total)
            short = feats[0].astype(BF16)
            qs[unit, :, cols] = short
            feat1[unit, :, cols] = feats[1]
            feat2[unit, :, cols] = feats[2]
            x_send[unit, :, cols] = (feats[1] * feats[2]).astype(BF16)
            g_send[unit, :, cols] = (
                g[unit, :, cols].astype(F32) * short.astype(F32)
            ).astype(BF16)

    def send_streams(at):
        for exchange, send, whole, helped in ((2, g_send, gf_recv, gh_recv), (1, x_send, xf_recv, xh_recv)):
            for j in range(1, S + 1):
                t = partner(at, j)
                skip = exchange == 2 and at < A and t >= A
                for n, count, base, recv in (
                    (2 * exchange, 0 if skip else plan.full[t], plan.full_base[t], whole),
                    (2 * exchange + 1, plan.help[t] if at < A else 0, plan.help_base[t], helped),
                ):
                    if count and t == at:
                        for i in range(count):
                            recv[at, i] = send[base + i]
                    elif count:
                        remote(
                            n, n, send.at[pl.ds(base, count)], recv.at[at, pl.ds(0, count)], t, me_c
                        ).start()

    each(send_streams)

    whole = (specs_f, half, first_ref, last_ref, twist_ref, twist_back_ref)
    helped = (specs_h, half // 2, first_h_ref, last_h_ref, twist_h_ref, twist_back_h_ref)

    def spectrum(kind, which, recv, count):
        specs, rows, first, _, twist, _ = kind
        sources, _, _, width = recv.shape
        per = width // LANES

        @pl.loop(0, count)
        def _(unit):
            @pl.loop(0, sources)
            def _(s):
                for r in range(per):
                    at = pl.multiple_of((s * per + r) * rb, rb)
                    rt[pl.ds(at, rb), :] = recv[s, unit, :, r * LANES : (r + 1) * LANES].astype(F32)

            @pl.loop(0, rb // 2, unroll=UNROLL)
            def _(p):
                pair = [rt[pl.ds(2 * p + h, rows, stride=rb), :] for h in range(2)]
                data = jnp.concatenate(pair, axis=1).astype(BF16)
                out = jnp.dot(first[...], data, preferred_element_type=F32)
                cos, sin = twist[0], twist[1]
                for h in range(2):
                    re = out[:rows, h * LANES : (h + 1) * LANES]
                    im = out[rows:, h * LANES : (h + 1) * LANES]
                    turned = jnp.concatenate(
                        [re * cos + im * sin, im * cos - re * sin], axis=1
                    ).astype(BF16)
                    specs[which, unit * rb + 2 * p + h] = jnp.dot(
                        turned, cols_ref[...], preferred_element_type=F32
                    ).astype(BF16)

    def convolve(kind, first_spec, second_spec, conj, send, unit):
        specs, rows, _, last, _, twist = kind
        targets, _, _, width = send.shape
        per = width // LANES

        @pl.loop(0, rb // 2, unroll=UNROLL)
        def _(p):
            parts = []
            cos, sin = twist[0], twist[1]
            for h in range(2):
                a = specs[first_spec, unit * rb + 2 * p + h].astype(F32)
                b = specs[second_spec, unit * rb + 2 * p + h].astype(F32)
                ar, ai, br, bi = a[:, :LANES], a[:, LANES:], b[:, :LANES], b[:, LANES:]
                if conj:
                    re, im = ar * br + ai * bi, ar * bi - ai * br
                else:
                    re, im = ar * br - ai * bi, ar * bi + ai * br
                prod = jnp.concatenate([re, im], axis=1).astype(BF16)
                back = jnp.dot(prod, cols_back_ref[...], preferred_element_type=F32)
                re, im = back[:, :LANES], back[:, LANES:]
                parts.append(
                    jnp.concatenate([re * cos - im * sin, im * cos + re * sin], axis=0)
                )
            data = jnp.concatenate(parts, axis=1).astype(BF16)
            out = jnp.dot(last[...], data, preferred_element_type=F32)
            for h in range(2):
                rt[pl.ds(2 * p + h, rows, stride=rb), :] = out[:, h * LANES : (h + 1) * LANES]

        @pl.loop(0, targets)
        def _(s):
            for r in range(per):
                at = pl.multiple_of((s * per + r) * rb, rb)
                send[s, unit, :, r * LANES : (r + 1) * LANES] = rt[pl.ds(at, rb), :].astype(BF16)

    def take(n, ref, *counts):
        where = tuple(pl.ds(0, count) for count in counts)
        if min(counts) > 0:
            pltpu.make_async_copy(ref.at[where], ref.at[where], rsem.at[n]).wait()

    def sent(n, ref, *counts):
        where = tuple(pl.ds(0, count) for count in counts)
        if min(counts) > 0:
            pltpu.make_async_copy(ref.at[where], ref.at[where], ssem.at[n]).wait()

    n_full, n_help = pick(plan.full), pick(plan.help)
    full_base, help_base = pick(plan.full_base), pick(plan.help_base)

    def give_whole(n, send, recv, unit, within):
        place = full_base + unit

        @pl.loop(1, A if within else S)
        def _(d):
            t = A + lax.rem(me_s - A + d, A) if within else partner_here(d)
            remote(2 * n, 2 * n, send.at[t, unit], recv.at[place], t, me_c).start()

    def give_helped(n, m, send, recv, unit):
        place = help_base + unit

        @pl.loop(1, A)
        def _(d):
            t = lax.rem(me_s + d, A)
            remote(2 * n + 1, m, send.at[t, unit], recv.at[place], t, me_c).start()

        recv[place] = send[me_s, unit]

    @pl.when(me_s >= A)
    def _():
        for s in range(A):
            gf_recv[s] = jnp.zeros(gf_recv.shape[1:], BF16)

        @pl.loop(na, NU)
        def _(unit):
            b_more[unit] = jnp.zeros(b_more.shape[1:], BF16)

    @pl.loop(0, na)
    def _(unit):
        b_more[unit] = jnp.zeros(b_more.shape[1:], BF16)

    def have_filter(at):
        for copy in own_filter(at):
            copy.wait()
        take(0, kf_recv, S * H - 1, plan.full[at])
        take(1, kh_recv, A * H - 1, plan.help[at])

    each(have_filter)
    for copy in table_copies:
        copy.wait()

    spectrum(whole, 0, kf_recv, n_full)
    spectrum(helped, 0, kh_recv, n_help)

    def have_grad(at):
        take(4, gf_recv, (S if at < A else A) - 1, plan.full[at])
        take(5, gh_recv, A - 1, plan.help[at])

    each(have_grad)
    spectrum(whole, 2, gf_recv, n_full)
    spectrum(helped, 2, gh_recv, n_help)

    @pl.loop(0, n_full)
    def _(unit):
        convolve(whole, 0, 2, True, bf_send, unit)
        give_whole(4, bf_send, b_recv, unit, False)
        b_recv[full_base + unit] = bf_send[me_s, unit]

    @pl.loop(0, n_help)
    def _(unit):
        convolve(helped, 0, 2, True, bh_send, unit)
        give_helped(4, 9, bh_send, b_more, unit)

    def have_mixer(at):
        take(2, xf_recv, S - 1, plan.full[at])
        take(3, xh_recv, A - 1, plan.help[at])

    each(have_mixer)
    spectrum(whole, 1, xf_recv, n_full)
    spectrum(helped, 1, xh_recv, n_help)

    @pl.loop(0, n_full)
    def _(unit):
        convolve(whole, 0, 1, False, yf_send, unit)

        @pl.when(me_s < A)
        def _():
            give_whole(3, yf_send, y_recv, unit, False)

        @pl.when(me_s >= A)
        def _():
            give_whole(3, yf_send, y_recv, unit, True)

        y_recv[full_base + unit] = yf_send[me_s, unit]

    @pl.loop(0, n_help)
    def _(unit):
        convolve(helped, 0, 1, False, yh_send, unit)
        give_helped(3, 6, yh_send, y_recv, unit)

    @pl.loop(0, n_full)
    def _(unit):
        convolve(whole, 1, 2, True, ff_send, unit)

    @pl.loop(0, n_help)
    def _(unit):
        convolve(helped, 1, 2, True, fh_send, unit)

    def own_result(at):
        copies = []
        for n, count, send, dst, place in (
            (2, plan.full[at], ff_send, gf_hbm, me_c * NU + plan.full_base[at]),
            (3, plan.help[at], fh_send, gf_more_hbm, me_c * nb + plan.help_base[at] - na),
        ):
            if count:
                copies.append(
                    pltpu.make_async_copy(
                        send.at[me, pl.ds(0, count)], dst.at[pl.ds(place, count)], own_sem.at[n]
                    )
                )
        return copies

    def send_result(at, begin, end):
        count, place = plan.full[at], me_c * NU + plan.full_base[at]
        for j in range(begin, end):
            if count:
                seq = partner(at, j)

                @pl.loop(1 if seq == at else 0, H)
                def _(e):
                    c = lax.rem(me_c + e, H)
                    remote(
                        10, 10, ff_send.at[seq * H + c, pl.ds(0, count)],
                        gf_hbm.at[pl.ds(place, count)], seq, c,
                    ).start()

    def send_helped(at):
        count, place = plan.help[at], me_c * nb + plan.help_base[at] - na
        if count:

            @pl.loop(1, A * H)
            def _(d):
                t = lax.rem(me + d, A * H)
                remote(
                    11, 11, fh_send.at[t, pl.ds(0, count)], gf_more_hbm.at[pl.ds(place, count)],
                    lax.div(t, H), lax.rem(t, H),
                ).start()

        for copy in own_result(at):
            copy.start()

    each(lambda at: send_result(at, 1, WAVES[0] + S))
    each(send_helped)

    def lane_sum(value):
        return jnp.sum(value, axis=1, keepdims=True)

    def fold(value):
        total = value[:, :LANES]
        for at in range(LANES, value.shape[1], LANES):
            total = total + value[:, at : at + LANES]
        return total

    def back_short(i, feats, stream, dst, left, unit, table):
        acc = [None] * 7
        for c in range(chunks):
            cols = slice(c * W, c * W + W)
            here = feats[unit, :, cols].astype(F32)
            if c + 1 < chunks:
                after = feats[unit, :, c * W + W : c * W + W + LANES].astype(F32)
            else:
                after = jnp.zeros((rb, LANES), F32)
            wide = jnp.concatenate([here, after], axis=1)
            value = stream[unit, :, cols].astype(F32)
            total = None
            for j in range(7):
                shifted = here if j == 0 else pltpu.roll(wide, W + LANES - j, 1)[:, :W]
                term = column(table, i, j) * shifted
                total = term if j == 0 else total + term
                piece = fold(shifted * value)
                if c == 0 and j > 0:
                    piece += jnp.where(lane < j, here[:, :LANES] * pltpu.roll(left, j, 1), 0.0)
                acc[j] = piece if c == 0 else acc[j] + piece
            dst[unit, :, cols] = total.astype(BF16)
        result = jnp.zeros((rb, LANES), F32)
        for j in range(7):
            result = jnp.where(lane == 8 * i + j, lane_sum(acc[j]), result)
        return result

    def last_block(i, feats, right, dst, unit, table):
        here = feats[unit, :, T - LANES : T].astype(F32)
        wide = jnp.concatenate([here, right], axis=1)
        total = column(table, i, 0) * here
        for j in range(1, 7):
            total += column(table, i, j) * pltpu.roll(wide, 2 * LANES - j, 1)[:, :LANES]
        dst[unit, :, T - LANES : T] = total.astype(BF16)

    def have_back(at):
        take(8, b_recv, NU - plan.full[at])
        if at < A:
            take(9, b_more, nb - plan.help[at])

    each(have_back)

    @pl.loop(0, NU)
    def _(unit):
        table = tab[unit]
        for c in range(chunks):
            cols = slice(c * W, c * W + W)
            inner = g[unit, :, cols].astype(F32) * qs[unit, :, cols].astype(F32)
            back = b_recv[unit, :, cols].astype(F32) + b_more[unit, :, cols].astype(F32)
            grad = (back + table[:, 7:8] * inner).astype(BF16).astype(F32)
            gf1[unit, :, cols] = (grad * feat2[unit, :, cols]).astype(BF16)
            gf2[unit, :, cols] = (grad * feat1[unit, :, cols]).astype(BF16)

    pack(3, ((gf1, 0, 0), (gf2, 0, 0)))

    @pl.when(me_s > 0)
    def _():
        halo_copy(3, -1).start()

    @pl.loop(0, NU)
    def _(unit):
        table = tab[unit]
        left = [unpack(n // 2, unit, n % 2, LANES - 6) for n in (1, 2)]
        one = back_short(1, gf1, k, gk, left[0], unit, table)
        two = back_short(2, gf2, v, gv, left[1], unit, table)
        part[unit] = one + two

    def have_long(at):
        take(6, y_recv, NU - plan.full[at] - plan.help[at])

    each(have_long)

    @pl.loop(0, NU)
    def _(unit):
        table = tab[unit]
        acc = jnp.zeros((rb, LANES), F32)
        for c in range(chunks):
            cols = slice(c * W, c * W + W)
            mixer = x_send[unit, :, cols].astype(F32)
            gate = y_recv[unit, :, cols].astype(F32) + table[:, 7:8] * mixer
            short = qs[unit, :, cols].astype(F32)
            grad = g[unit, :, cols].astype(F32)
            mixed[unit, :, cols] = (short * gate).astype(BF16)
            gf0[unit, :, cols] = (grad * gate).astype(BF16)
            acc += fold(grad * short * mixer)
        part[unit] += jnp.where(lane == 7, lane_sum(acc), 0.0)

    each(lambda at: send_result(at, WAVES[0] + S, WAVES[1] + S))
    pack(2, ((gf0, 0, 0),))

    @pl.when(me_s > 0)
    def _():
        halo_copy(2, -1).start()

    outs = [pltpu.make_async_copy(mixed, mixed_hbm, out_sem.at[0])]
    outs[0].start()

    @pl.loop(0, NU)
    def _(unit):
        left = unpack(0, unit, 0, LANES - 6)
        part[unit] += back_short(0, gf0, q, gq, left, unit, tab[unit])

    turned = jnp.transpose(part[...].reshape(NU * rb, LANES))
    lane8 = lax.broadcasted_iota(jnp.int32, (8, LANES), 1)

    def moved(block, shift):
        return pltpu.roll(block, shift % LANES, 1) if shift % LANES else block

    for grp in range(S):
        base = grp * G // LANES * LANES
        tile = jnp.zeros((8, LANES), F32)
        for i in range(3):
            block = turned[8 * i : 8 * i + 8, base : base + LANES]
            tile = jnp.where(lane8 // G == i, moved(block, i * G - grp * G), tile)
        sums_send[grp] = tile
    sums_recv[me_s] = sums_send[me_s]

    def sums_copy(n, src, dst, t):
        return pltpu.make_async_remote_copy(
            src_ref=src, dst_ref=dst.at[me_s], send_sem=ssem.at[n], recv_sem=rsem.at[n],
            device_id=(t, me_c), device_id_type=MESH,
        )

    @pl.loop(1, S)
    def _(d):
        t = lax.rem(me_s + d, S)
        sums_copy(12, sums_send.at[t], sums_recv, t).start()

    each(lambda at: send_result(at, WAVES[1] + S, S + 1))

    for which in (2, 3):

        @pl.when(me_s < S - 1)
        def _():
            halo_copy(which, 1).wait_recv()

        @pl.when(me_s == S - 1)
        def _():
            halo_recv[which] = jnp.zeros(halo_recv.shape[1:], BF16)

    @pl.loop(0, NU)
    def _(unit):
        table = tab[unit]
        last_block(0, gf0, unpack(2, unit, 0, 0), gq, unit, table)
        last_block(1, gf1, unpack(3, unit, 0, 0), gk, unit, table)
        last_block(2, gf2, unpack(3, unit, 1, 0), gv, unit, table)

    for n, (src, dst) in enumerate(((gq, gq_hbm), (gk, gk_hbm), (gv, gv_hbm))):
        outs.append(pltpu.make_async_copy(src, dst, out_sem.at[n + 1]))
        outs[-1].start()

    take(12, sums_recv, S - 1)
    total = sums_recv[0]
    for s in range(1, S):
        total = total + sums_recv[s]
    total_send[...] = total * scale_root
    total_recv[me_s] = total_send[...]

    @pl.loop(1, S)
    def _(d):
        sums_copy(13, total_send, total_recv, lax.rem(me_s + d, S)).start()

    take(13, total_recv, S - 1)
    for base in range(0, S * G, LANES):
        for i in range(3):
            block = jnp.zeros((8, LANES), F32)
            for grp in range(base // G, min(S * G, base + LANES) // G):
                mine = lane8 // G == (grp * G - base) // G
                block = jnp.where(mine, moved(total_recv[grp], grp * G - i * G), block)
            short_out[i, :, base : base + LANES] = block[0:7]
            if i == 0:
                skip_out[:, base : base + LANES] = block[7:8]

    def all_sent(at):
        full, helps = plan.full[at], plan.help[at]
        early = at < A
        sent(0, filt_hbm, NU * H - full)
        sent(2, x_send, NU - full)
        sent(4, g_send, (na if early else NU) - full)
        sent(6, yf_send, (S if early else A) - 1, full)
        sent(8, bf_send, S - 1, full)
        sent(10, ff_send, S * H - 1, full)
        if early:
            sent(1, filt_hbm, nb * H - helps)
            sent(3, x_send, nb - helps)
            sent(5, g_send, nb - helps)
            sent(7, yh_send, A - 1, helps)
            sent(9, bh_send, A - 1, helps)
            sent(11, fh_send, A * H - 1, helps)
        for copy in own_result(at):
            copy.wait()
        take(10, gf_hbm, H * NU - full)
        if early:
            take(11, gf_more_hbm, H * nb - helps)

    sent(12, sums_recv, S - 1)
    sent(13, total_recv, S - 1)

    @pl.when(me_s < S - 1)
    def _():
        halo_copy(0, 1).wait_send()

    for which in (2, 3):

        @pl.when(me_s > 0)
        def _():
            halo_copy(which, -1).wait_send()

    for copy in outs:
        copy.wait()
    each(all_sent)


def hand_on(plan, arrays, more):
    pieces = [4 if a.size > 2**17 else 1 for a in arrays]
    count = len(arrays)
    parts = [a.shape[0] // cuts for a, cuts in zip(arrays, pieces)]
    H, NU, na, nb = plan.H, plan.NU, plan.na, plan.nb

    def body(*refs):
        sources, more_ref, dests = refs[:count], refs[count], refs[count + 1 : 2 * count + 1]
        held = refs[2 * count + 1 : 3 * count + 1]
        more_held, sem_in, sem_out, sem_more = refs[3 * count + 1 :]
        arriving, leaving = [], []
        order = [count - 1] + list(range(count - 1))
        for i in order:
            for at in range(pieces[i]):
                where = pl.ds(at * parts[i], parts[i])
                n = len(arriving)
                arriving.append(
                    pltpu.make_async_copy(sources[i].at[where], held[i].at[where], sem_in.at[n])
                )
                leaving.append(
                    pltpu.make_async_copy(held[i].at[where], dests[i].at[where], sem_out.at[n])
                )
        first_half = lax.axis_index("seq") < plan.A
        extra = pltpu.make_async_copy(more_ref, more_held, sem_more)

        @pl.when(first_half)
        def _():
            extra.start()

        for copy in arriving:
            copy.start()
        last = pieces[-1]
        for one, two in zip(arriving[last:], leaving[last:]):
            one.wait()
            two.start()
        for one in arriving[:last]:
            one.wait()

        @pl.when(first_half)
        def _():
            extra.wait()
            for c in range(H):

                @pl.loop(0, nb)
                def _(i):
                    total = held[-1][c * NU + na + i].astype(F32) + more_held[c * nb + i].astype(F32)
                    held[-1][c * NU + na + i] = total.astype(BF16)

        for two in leaving[:last]:
            two.start()
        for copy in leaving:
            copy.wait()

    spec = pl.BlockSpec(memory_space=pl.ANY)
    return pl.pallas_call(
        body,
        out_shape=tuple(jax.ShapeDtypeStruct(a.shape, a.dtype) for a in arrays),
        in_specs=[spec] * (count + 1),
        out_specs=(spec,) * count,
        scratch_shapes=[pltpu.VMEM(a.shape, a.dtype) for a in arrays + (more,)]
        + [pltpu.SemaphoreType.DMA((sum(pieces),))] * 2
        + [pltpu.SemaphoreType.DMA],
        compiler_params=pltpu.CompilerParams(vmem_limit_bytes=58 * 2**20),
    )(*arrays, more)


def per_device(query_proj, key_proj, value_proj, short_taps, skip_gain, filter_raw, grad_out):
    channels, T = query_proj.shape
    S = lax.axis_size("seq")
    H = lax.axis_size("chan")
    plan = Plan(S, H, channels, S * T)
    A, NU, rb, FT, nf, nh, nb = plan.A, plan.NU, plan.rb, plan.FT, plan.nf, plan.nh, plan.nb
    half = S * T // LANES
    split = lambda a: a.reshape(NU, rb, T)
    first, last, cols, cols_back, twist, twist_back = make_tables(S * T, S * T)
    first_h, last_h, _, _, twist_h, twist_back_h = make_tables(A * T, S * T)
    tables = (first, last, twist, twist_back, first_h, last_h, twist_h, twist_back_h, cols, cols_back)
    any_spec = pl.BlockSpec(memory_space=pl.ANY)
    vmem = pl.BlockSpec(memory_space=pltpu.VMEM)
    stream = jax.ShapeDtypeStruct((NU, rb, T), BF16)
    held = pltpu.VMEM((NU, rb, T), BF16)
    wide = pltpu.VMEM((NU, rb, T), F32)
    edge = pltpu.VMEM((4, NU // 8, rb, LANES), BF16)
    small = pltpu.VMEM((NU, rb, LANES), F32)
    outs = pl.pallas_call(
        functools.partial(kernel, plan),
        out_shape=(
            stream, stream, stream, stream,
            jax.ShapeDtypeStruct((3, 7, channels), F32),
            jax.ShapeDtypeStruct((1, channels), F32),
            jax.ShapeDtypeStruct((H * NU, rb, FT), BF16),
            jax.ShapeDtypeStruct((H * nb, rb, FT), BF16),
        ),
        in_specs=[any_spec] * 4 + [vmem] * 2 + [any_spec] + [(any_spec,) * len(tables)],
        out_specs=(any_spec,) * 4 + (vmem,) * 2 + (any_spec,) * 2,
        scratch_shapes=[
            tuple(pltpu.VMEM(a.shape, a.dtype) for a in tables),
            held, held, held, held,
            pltpu.VMEM((LANES, channels), F32),
            small, small,
            held, wide, wide,
            edge, edge,
            held, held,
            pltpu.VMEM((S * H, nf, rb, FT), BF16),
            pltpu.VMEM((S, nf, rb, T), BF16),
            pltpu.VMEM((S, nf, rb, T), BF16),
            pltpu.VMEM((A * H, nh, rb, FT), BF16),
            pltpu.VMEM((A, nh, rb, T), BF16),
            pltpu.VMEM((A, nh, rb, T), BF16),
            pltpu.VMEM((half * rb, LANES), F32),
            pltpu.VMEM((3, nf * rb, half, 2 * LANES), BF16),
            pltpu.VMEM((3, nh * rb, half // 2, 2 * LANES), BF16),
            pltpu.VMEM((S, nf, rb, T), BF16),
            pltpu.VMEM((S, nf, rb, T), BF16),
            pltpu.VMEM((S * H, nf, rb, FT), BF16),
            pltpu.VMEM((A, nh, rb, T), BF16),
            pltpu.VMEM((A, nh, rb, T), BF16),
            pltpu.VMEM((A * H, nh, rb, FT), BF16),
            held, held, held,
            held, held, held,
            held, held, held, held,
            pltpu.VMEM((S, 8, LANES), F32),
            pltpu.VMEM((S, 8, LANES), F32),
            pltpu.VMEM((8, LANES), F32),
            pltpu.VMEM((S, 8, LANES), F32),
            pltpu.SemaphoreType.DMA((len(tables),)),
            pltpu.SemaphoreType.DMA((4,)),
            pltpu.SemaphoreType.DMA((4,)),
            pltpu.SemaphoreType.DMA((4,)),
            pltpu.SemaphoreType.DMA((4,)),
            pltpu.SemaphoreType.DMA((4,)),
            pltpu.SemaphoreType.DMA((14,)),
            pltpu.SemaphoreType.DMA((14,)),
        ],
        compiler_params=pltpu.CompilerParams(
            collective_id=0, has_side_effects=True, vmem_limit_bytes=60 * 2**20
        ),
        cost_estimate=pl.CostEstimate(
            flops=6 * 4 * channels * T * S * 16, bytes_accessed=12 * channels * T * 2, transcendentals=0
        ),
    )(
        split(query_proj), split(key_proj), split(value_proj), split(grad_out),
        short_taps, skip_gain.reshape(1, channels), filter_raw.reshape(H * NU, rb, FT),
        tables,
    )
    mixed, gq, gk, gv, short, skip, gf = hand_on(plan, outs[:-1], outs[-1])
    back = lambda a: a.reshape(channels, T)
    return (
        back(mixed), back(gq), back(gk), back(gv), short, skip.reshape(channels),
        gf.reshape(H * NU * rb, FT),
    )


def solution(mesh):
    placed = (
        P("chan", "seq"),
        P("chan", "seq"),
        P("chan", "seq"),
        P(None, None, "chan"),
        P("chan"),
        P(None, ("seq", "chan")),
        P("chan", "seq"),
    )
    return jax.shard_map(
        per_device,
        mesh=mesh,
        in_specs=placed,
        out_specs=(
            P("chan", "seq"),
            P("chan", "seq"),
            P("chan", "seq"),
            P("chan", "seq"),
            P(None, None, "chan"),
            P("chan"),
            P(None, ("seq", "chan")),
        ),
        check_vma=False,
    )
```

```python
import functools
import math

import jax
import jax.numpy as jnp
import numpy as np
from jax import lax
from jax.experimental import pallas as pl
from jax.experimental.pallas import tpu as pltpu
from jax.sharding import PartitionSpec as P
import ml_dtypes

MESH = pl.DeviceIdType.MESH
F32 = jnp.float32
BF16 = jnp.bfloat16
LANES = 128
UNROLL = 4
WAVES = (-4, -2)


class Plan:
    def __init__(self, seq, chan, channels, length):
        self.S, self.H, self.A = seq, chan, seq // 2
        self.rb = math.gcd(channels, 16 if channels >= 256 else 8)
        self.NU = channels // self.rb
        self.nb = self.NU * 5 // 8
        self.na = self.NU - self.nb
        spread = lambda n, m: [n // m + (i < n % m) for i in range(m)]
        if (seq, self.NU) == (8, 16):
            first, second, self.help = [1, 1, 2, 2], [3, 2, 3, 2], [3, 3, 2, 2]
        else:
            first, second = spread(self.na, self.A), spread(self.nb, self.A)
            self.help = spread(self.nb, self.A)
        self.full = first + second
        self.help = self.help + [0] * self.A
        self.full_base = [sum(self.full[:i]) for i in range(seq)]
        self.help_base = [self.na + sum(self.help[:i]) for i in range(seq)]
        self.nf, self.nh = max(self.full), max(self.help)
        self.T = length // seq
        self.FT = self.T // chan


def make_tables(length, whole):
    points = 2 * length
    rows = points // LANES
    half = rows // 2
    n1 = np.arange(half, dtype=np.float64)
    k1 = np.arange(half, dtype=np.float64) + 0.5
    n2 = np.arange(LANES, dtype=np.float64)
    angle = 2 * np.pi * np.outer(k1, n1) / rows
    first = np.concatenate([np.cos(angle), -np.sin(angle)], axis=0)
    last = np.concatenate([np.cos(angle.T), -np.sin(angle.T)], axis=1)
    angle = 2 * np.pi * np.outer(n2, n2) / LANES
    c, s = np.cos(angle), np.sin(angle)
    cols = np.block([[c, -s], [s, c]])
    cols_back = np.block([[c, s], [-s, c]])
    angle = 2 * np.pi * np.outer(k1, n2) / points
    scale = (2.0 / points) / math.sqrt(whole)
    twist = np.stack([np.cos(angle), np.sin(angle)])
    as16 = lambda a: jnp.asarray(a.astype(np.float32).astype(ml_dtypes.bfloat16))
    as32 = lambda a: jnp.asarray(a.astype(np.float32))
    return as16(first), as16(last), as16(cols), as16(cols_back), as32(twist), as32(twist * scale)


def kernel(
    plan,
    q_hbm, k_hbm, v_hbm, g_hbm, taps_ref, skip_ref, filt_hbm,
    tables_hbm,
    mixed_hbm, gq_hbm, gk_hbm, gv_hbm, short_out, skip_out, gf_hbm, gf_more_hbm,
    tables, q, k, v, g, tab_t, tab, part, qs, feat1, feat2,
    halo_send, halo_recv, x_send, g_send,
    kf_recv, xf_recv, gf_recv, kh_recv, xh_recv, gh_recv,
    rt, specs_f, specs_h, yf_send, bf_send, ff_send, yh_send, bh_send, fh_send,
    y_recv, b_recv, b_more,
    gf0, gf1, gf2, mixed, gq, gk, gv, sums_send, sums_recv, total_send, total_recv,
    table_sem, in_sem, out_sem, own_sem, halo_ssem, halo_rsem, ssem, rsem,
):
    S, H, A, NU, rb, T, FT = plan.S, plan.H, plan.A, plan.NU, plan.rb, plan.T, plan.FT
    na, nb = plan.na, plan.nb
    G = NU * rb // S
    half = S * T // LANES
    W = min(512, T)
    chunks = T // W
    ndev = S * H
    me_s = lax.axis_index("seq")
    me_c = lax.axis_index("chan")
    me = me_s * H + me_c
    scale_root = 1.0 / math.sqrt(S * T)

    (
        first_ref, last_ref, twist_ref, twist_back_ref,
        first_h_ref, last_h_ref, twist_h_ref, twist_back_h_ref, cols_ref, cols_back_ref,
    ) = tables
    table_copies = [
        pltpu.make_async_copy(src, dst, table_sem.at[i])
        for i, (src, dst) in enumerate(zip(tables_hbm, tables))
    ]

    ins = [
        pltpu.make_async_copy(src, dst, in_sem.at[i])
        for i, (src, dst) in enumerate(((q_hbm, q), (k_hbm, k), (v_hbm, v), (g_hbm, g)))
    ]
    for copy in ins:
        copy.start()
    barrier = pltpu.get_barrier_semaphore()

    @pl.loop(1, ndev)
    def _(d):
        t = lax.rem(me + d, ndev)
        pl.semaphore_signal(
            barrier, inc=1, device_id=(t // H, lax.rem(t, H)), device_id_type=MESH
        )

    tab_t[...] = jnp.zeros_like(tab_t)
    for i in range(3):
        tab_t[8 * i : 8 * i + 7, :] = taps_ref[i].astype(F32)
    tab_t[7:8, :] = skip_ref[...]
    tab[...] = jnp.transpose(tab_t[...]).reshape(tab.shape)

    lane = lax.broadcasted_iota(jnp.int32, (rb, LANES), 1)
    for copy in ins[:3]:
        copy.wait()

    def pack(which, edges):
        for hb in range(NU // 8):
            packed = jnp.zeros((rb, LANES), F32)
            for slot in range(8):
                for n, (ref, at, offset) in enumerate(edges):
                    block = ref[hb * 8 + slot, :, at : at + LANES].astype(F32)
                    begin = 16 * slot + 6 * n
                    shift = (begin - offset) % LANES
                    if shift:
                        block = pltpu.roll(block, shift, 1)
                    packed = jnp.where((lane >= begin) & (lane < begin + 6), block, packed)
            halo_send[which, hb] = packed.astype(BF16)

    def unpack(which, unit, n, offset):
        packed = halo_recv[which, lax.div(unit, 8)].astype(F32)
        shift = lax.rem(offset - 6 * n - 16 * lax.rem(unit, 8) + 2 * LANES, LANES)
        return pltpu.roll(packed, shift, 1)

    pack(0, ((q, T - LANES, LANES - 6), (k, T - LANES, LANES - 6)))
    pack(1, ((v, T - LANES, LANES - 6),))
    pl.semaphore_wait(barrier, ndev - 1)

    def halo_copy(which, step):
        target = lax.rem(me_s + step + S, S)
        blocks = pl.ds(0, 2) if which == 0 else pl.ds(which, 1)
        return pltpu.make_async_remote_copy(
            src_ref=halo_send.at[blocks], dst_ref=halo_recv.at[blocks],
            send_sem=halo_ssem.at[which], recv_sem=halo_rsem.at[which],
            device_id=(target, me_c), device_id_type=MESH,
        )

    @pl.when(me_s < S - 1)
    def _():
        halo_copy(0, 1).start()

    def partner(at, j):
        d = (j + 1) % S
        return ((at // A + 1 + d % 2) % 2) * A + (at % A + d // 2) % A

    def partner_here(j):
        d = lax.rem(j + 1, S)
        side = lax.rem(lax.div(me_s, A) + 1 + lax.rem(d, 2), 2)
        return side * A + lax.rem(lax.rem(me_s, A) + lax.div(d, 2), A)

    def each(act):
        for at in range(S):

            @pl.when(me_s == at)
            def _():
                act(at)

    def pick(values):
        return sum(jnp.where(me_s == i, n, 0) for i, n in enumerate(values))

    def remote(n, m, src, dst, seq, chan):
        return pltpu.make_async_remote_copy(
            src_ref=src, dst_ref=dst, send_sem=ssem.at[n], recv_sem=rsem.at[m],
            device_id=(seq, chan), device_id_type=MESH,
        )

    def own_filter(at):
        copies = []
        for n, count, base, recv in (
            (0, plan.full[at], plan.full_base[at], kf_recv),
            (1, plan.help[at], plan.help_base[at], kh_recv),
        ):
            if count:
                copies.append(
                    pltpu.make_async_copy(
                        filt_hbm.at[pl.ds(me_c * NU + base, count)],
                        recv.at[me, pl.ds(0, count)],
                        own_sem.at[n],
                    )
                )
        return copies

    def send_filter(at):
        for j in range(1, S + 1):
            t = partner(at, j)
            for n, count, base, recv in (
                (0, plan.full[t], plan.full_base[t], kf_recv),
                (1, plan.help[t] if at < A else 0, plan.help_base[t], kh_recv),
            ):
                if count:

                    @pl.loop(1 if t == at else 0, H)
                    def _(e):
                        c = lax.rem(me_c + e, H)
                        remote(
                            n, n, filt_hbm.at[pl.ds(c * NU + base, count)],
                            recv.at[me, pl.ds(0, count)], t, c,
                        ).start()

        for copy in own_filter(at):
            copy.start()

    each(send_filter)
    for copy in table_copies:
        copy.start()


    ins[3].wait()

    @pl.when(me_s > 0)
    def _():
        halo_copy(0, -1).wait_recv()

    @pl.when(me_s == 0)
    def _():
        halo_recv[0:2] = jnp.zeros((2,) + halo_recv.shape[1:], BF16)

    def column(table, i, j):
        return table[:, 8 * i + j : 8 * i + j + 1]

    @pl.loop(0, NU)
    def _(unit):
        table = tab[unit]
        lefts = [unpack(n // 2, unit, n % 2, LANES - 6) for n in range(3)]
        for c in range(chunks):
            cols = slice(c * W, c * W + W)
            feats = []
            for i, stream in enumerate((q, k, v)):
                here = stream[unit, :, cols].astype(F32)
                wide = jnp.concatenate([lefts[i], here], axis=1)
                total = column(table, i, 0) * here
                for j in range(1, 7):
                    total += column(table, i, j) * pltpu.roll(wide, j, 1)[:, LANES:]
                lefts[i] = here[:, W - LANES :]
                feats.append(total)
            short = feats[0].astype(BF16)
            qs[unit, :, cols] = short
            feat1[unit, :, cols] = feats[1]
            feat2[unit, :, cols] = feats[2]
            x_send[unit, :, cols] = (feats[1] * feats[2]).astype(BF16)
            g_send[unit, :, cols] = (
                g[unit, :, cols].astype(F32) * short.astype(F32)
            ).astype(BF16)

    def send_streams(at):
        for exchange, send, whole, helped in ((2, g_send, gf_recv, gh_recv), (1, x_send, xf_recv, xh_recv)):
            for j in range(1, S + 1):
                t = partner(at, j)
                skip = exchange == 2 and at < A and t >= A
                for n, count, base, recv in (
                    (2 * exchange, 0 if skip else plan.full[t], plan.full_base[t], whole),
                    (2 * exchange + 1, plan.help[t] if at < A else 0, plan.help_base[t], helped),
                ):
                    if count and t == at:
                        for i in range(count):
                            recv[at, i] = send[base + i]
                    elif count:
                        remote(
                            n, n, send.at[pl.ds(base, count)], recv.at[at, pl.ds(0, count)], t, me_c
                        ).start()

    each(send_streams)

    whole = (specs_f, half, first_ref, last_ref, twist_ref, twist_back_ref)
    helped = (specs_h, half // 2, first_h_ref, last_h_ref, twist_h_ref, twist_back_h_ref)

    def spectrum(kind, which, recv, count):
        specs, rows, first, _, twist, _ = kind
        sources, _, _, width = recv.shape
        per = width // LANES

        @pl.loop(0, count)
        def _(unit):
            @pl.loop(0, sources)
            def _(s):
                for r in range(per):
                    at = pl.multiple_of((s * per + r) * rb, rb)
                    rt[pl.ds(at, rb), :] = recv[s, unit, :, r * LANES : (r + 1) * LANES].astype(F32)

            @pl.loop(0, rb // 2, unroll=UNROLL)
            def _(p):
                pair = [rt[pl.ds(2 * p + h, rows, stride=rb), :] for h in range(2)]
                data = jnp.concatenate(pair, axis=1).astype(BF16)
                out = jnp.dot(first[...], data, preferred_element_type=F32)
                cos, sin = twist[0], twist[1]
                for h in range(2):
                    re = out[:rows, h * LANES : (h + 1) * LANES]
                    im = out[rows:, h * LANES : (h + 1) * LANES]
                    turned = jnp.concatenate(
                        [re * cos + im * sin, im * cos - re * sin], axis=1
                    ).astype(BF16)
                    specs[which, unit * rb + 2 * p + h] = jnp.dot(
                        turned, cols_ref[...], preferred_element_type=F32
                    ).astype(BF16)

    def convolve(kind, first_spec, second_spec, conj, send, unit):
        specs, rows, _, last, _, twist = kind
        targets, _, _, width = send.shape
        per = width // LANES

        @pl.loop(0, rb // 2, unroll=UNROLL)
        def _(p):
            parts = []
            cos, sin = twist[0], twist[1]
            for h in range(2):
                a = specs[first_spec, unit * rb + 2 * p + h].astype(F32)
                b = specs[second_spec, unit * rb + 2 * p + h].astype(F32)
                ar, ai, br, bi = a[:, :LANES], a[:, LANES:], b[:, :LANES], b[:, LANES:]
                if conj:
                    re, im = ar * br + ai * bi, ar * bi - ai * br
                else:
                    re, im = ar * br - ai * bi, ar * bi + ai * br
                prod = jnp.concatenate([re, im], axis=1).astype(BF16)
                back = jnp.dot(prod, cols_back_ref[...], preferred_element_type=F32)
                re, im = back[:, :LANES], back[:, LANES:]
                parts.append(
                    jnp.concatenate([re * cos - im * sin, im * cos + re * sin], axis=0)
                )
            data = jnp.concatenate(parts, axis=1).astype(BF16)
            out = jnp.dot(last[...], data, preferred_element_type=F32)
            for h in range(2):
                rt[pl.ds(2 * p + h, rows, stride=rb), :] = out[:, h * LANES : (h + 1) * LANES]

        @pl.loop(0, targets)
        def _(s):
            for r in range(per):
                at = pl.multiple_of((s * per + r) * rb, rb)
                send[s, unit, :, r * LANES : (r + 1) * LANES] = rt[pl.ds(at, rb), :].astype(BF16)

    def take(n, ref, *counts):
        where = tuple(pl.ds(0, count) for count in counts)
        if min(counts) > 0:
            pltpu.make_async_copy(ref.at[where], ref.at[where], rsem.at[n]).wait()

    def sent(n, ref, *counts):
        where = tuple(pl.ds(0, count) for count in counts)
        if min(counts) > 0:
            pltpu.make_async_copy(ref.at[where], ref.at[where], ssem.at[n]).wait()

    n_full, n_help = pick(plan.full), pick(plan.help)
    full_base, help_base = pick(plan.full_base), pick(plan.help_base)

    def give_whole(n, send, recv, unit, within):
        place = full_base + unit

        @pl.loop(1, A if within else S)
        def _(d):
            t = A + lax.rem(me_s - A + d, A) if within else partner_here(d)
            remote(2 * n, 2 * n, send.at[t, unit], recv.at[place], t, me_c).start()

    def give_helped(n, m, send, recv, unit):
        place = help_base + unit

        @pl.loop(1, A)
        def _(d):
            t = lax.rem(me_s + d, A)
            remote(2 * n + 1, m, send.at[t, unit], recv.at[place], t, me_c).start()

        recv[place] = send[me_s, unit]

    @pl.when(me_s >= A)
    def _():
        for s in range(A):
            gf_recv[s] = jnp.zeros(gf_recv.shape[1:], BF16)

        @pl.loop(na, NU)
        def _(unit):
            b_more[unit] = jnp.zeros(b_more.shape[1:], BF16)

    @pl.loop(0, na)
    def _(unit):
        b_more[unit] = jnp.zeros(b_more.shape[1:], BF16)

    def have_filter(at):
        for copy in own_filter(at):
            copy.wait()
        take(0, kf_recv, S * H - 1, plan.full[at])
        take(1, kh_recv, A * H - 1, plan.help[at])

    each(have_filter)
    for copy in table_copies:
        copy.wait()

    spectrum(whole, 0, kf_recv, n_full)
    spectrum(helped, 0, kh_recv, n_help)

    def have_grad(at):
        take(4, gf_recv, (S if at < A else A) - 1, plan.full[at])
        take(5, gh_recv, A - 1, plan.help[at])

    each(have_grad)
    spectrum(whole, 2, gf_recv, n_full)
    spectrum(helped, 2, gh_recv, n_help)

    @pl.loop(0, n_full)
    def _(unit):
        convolve(whole, 0, 2, True, bf_send, unit)
        give_whole(4, bf_send, b_recv, unit, False)
        b_recv[full_base + unit] = bf_send[me_s, unit]

    @pl.loop(0, n_help)
    def _(unit):
        convolve(helped, 0, 2, True, bh_send, unit)
        give_helped(4, 9, bh_send, b_more, unit)

    def have_mixer(at):
        take(2, xf_recv, S - 1, plan.full[at])
        take(3, xh_recv, A - 1, plan.help[at])

    each(have_mixer)
    spectrum(whole, 1, xf_recv, n_full)
    spectrum(helped, 1, xh_recv, n_help)

    @pl.loop(0, n_full)
    def _(unit):
        convolve(whole, 0, 1, False, yf_send, unit)

        @pl.when(me_s < A)
        def _():
            give_whole(3, yf_send, y_recv, unit, False)

        @pl.when(me_s >= A)
        def _():
            give_whole(3, yf_send, y_recv, unit, True)

        y_recv[full_base + unit] = yf_send[me_s, unit]

    @pl.loop(0, n_help)
    def _(unit):
        convolve(helped, 0, 1, False, yh_send, unit)
        give_helped(3, 6, yh_send, y_recv, unit)

    @pl.loop(0, n_full)
    def _(unit):
        convolve(whole, 1, 2, True, ff_send, unit)

    @pl.loop(0, n_help)
    def _(unit):
        convolve(helped, 1, 2, True, fh_send, unit)

    def own_result(at):
        copies = []
        for n, count, send, dst, place in (
            (2, plan.full[at], ff_send, gf_hbm, me_c * NU + plan.full_base[at]),
            (3, plan.help[at], fh_send, gf_more_hbm, me_c * nb + plan.help_base[at] - na),
        ):
            if count:
                copies.append(
                    pltpu.make_async_copy(
                        send.at[me, pl.ds(0, count)], dst.at[pl.ds(place, count)], own_sem.at[n]
                    )
                )
        return copies

    def send_result(at, begin, end):
        count, place = plan.full[at], me_c * NU + plan.full_base[at]
        for j in range(begin, end):
            if count:
                seq = partner(at, j)

                @pl.loop(1 if seq == at else 0, H)
                def _(e):
                    c = lax.rem(me_c + e, H)
                    remote(
                        10, 10, ff_send.at[seq * H + c, pl.ds(0, count)],
                        gf_hbm.at[pl.ds(place, count)], seq, c,
                    ).start()

    def send_helped(at):
        count, place = plan.help[at], me_c * nb + plan.help_base[at] - na
        if count:

            @pl.loop(1, A * H)
            def _(d):
                t = lax.rem(me + d, A * H)
                remote(
                    11, 11, fh_send.at[t, pl.ds(0, count)], gf_more_hbm.at[pl.ds(place, count)],
                    lax.div(t, H), lax.rem(t, H),
                ).start()

        for copy in own_result(at):
            copy.start()

    each(lambda at: send_result(at, 1, WAVES[0] + S))
    each(send_helped)

    def lane_sum(value):
        return jnp.sum(value, axis=1, keepdims=True)

    def fold(value):
        total = value[:, :LANES]
        for at in range(LANES, value.shape[1], LANES):
            total = total + value[:, at : at + LANES]
        return total

    def back_short(i, feats, stream, dst, left, unit, table):
        acc = [None] * 7
        for c in range(chunks):
            cols = slice(c * W, c * W + W)
            here = feats[unit, :, cols].astype(F32)
            if c + 1 < chunks:
                after = feats[unit, :, c * W + W : c * W + W + LANES].astype(F32)
            else:
                after = jnp.zeros((rb, LANES), F32)
            wide = jnp.concatenate([here, after], axis=1)
            value = stream[unit, :, cols].astype(F32)
            total = None
            for j in range(7):
                shifted = here if j == 0 else pltpu.roll(wide, W + LANES - j, 1)[:, :W]
                term = column(table, i, j) * shifted
                total = term if j == 0 else total + term
                piece = fold(shifted * value)
                if c == 0 and j > 0:
                    piece += jnp.where(lane < j, here[:, :LANES] * pltpu.roll(left, j, 1), 0.0)
                acc[j] = piece if c == 0 else acc[j] + piece
            dst[unit, :, cols] = total.astype(BF16)
        result = jnp.zeros((rb, LANES), F32)
        for j in range(7):
            result = jnp.where(lane == 8 * i + j, lane_sum(acc[j]), result)
        return result

    def last_block(i, feats, right, dst, unit, table):
        here = feats[unit, :, T - LANES : T].astype(F32)
        wide = jnp.concatenate([here, right], axis=1)
        total = column(table, i, 0) * here
        for j in range(1, 7):
            total += column(table, i, j) * pltpu.roll(wide, 2 * LANES - j, 1)[:, :LANES]
        dst[unit, :, T - LANES : T] = total.astype(BF16)

    def have_back(at):
        take(8, b_recv, NU - plan.full[at])
        if at < A:
            take(9, b_more, nb - plan.help[at])

    each(have_back)

    @pl.loop(0, NU)
    def _(unit):
        table = tab[unit]
        for c in range(chunks):
            cols = slice(c * W, c * W + W)
            inner = g[unit, :, cols].astype(F32) * qs[unit, :, cols].astype(F32)
            back = b_recv[unit, :, cols].astype(F32) + b_more[unit, :, cols].astype(F32)
            grad = (back + table[:, 7:8] * inner).astype(BF16).astype(F32)
            gf1[unit, :, cols] = (grad * feat2[unit, :, cols]).astype(BF16)
            gf2[unit, :, cols] = (grad * feat1[unit, :, cols]).astype(BF16)

    pack(3, ((gf1, 0, 0), (gf2, 0, 0)))

    @pl.when(me_s > 0)
    def _():
        halo_copy(3, -1).start()

    @pl.loop(0, NU)
    def _(unit):
        table = tab[unit]
        left = [unpack(n // 2, unit, n % 2, LANES - 6) for n in (1, 2)]
        one = back_short(1, gf1, k, gk, left[0], unit, table)
        two = back_short(2, gf2, v, gv, left[1], unit, table)
        part[unit] = one + two

    def have_long(at):
        take(6, y_recv, NU - plan.full[at] - plan.help[at])

    each(have_long)

    @pl.loop(0, NU)
    def _(unit):
        table = tab[unit]
        acc = jnp.zeros((rb, LANES), F32)
        for c in range(chunks):
            cols = slice(c * W, c * W + W)
            mixer = x_send[unit, :, cols].astype(F32)
            gate = y_recv[unit, :, cols].astype(F32) + table[:, 7:8] * mixer
            short = qs[unit, :, cols].astype(F32)
            grad = g[unit, :, cols].astype(F32)
            mixed[unit, :, cols] = (short * gate).astype(BF16)
            gf0[unit, :, cols] = (grad * gate).astype(BF16)
            acc += fold(grad * short * mixer)
        part[unit] += jnp.where(lane == 7, lane_sum(acc), 0.0)

    each(lambda at: send_result(at, WAVES[0] + S, WAVES[1] + S))
    pack(2, ((gf0, 0, 0),))

    @pl.when(me_s > 0)
    def _():
        halo_copy(2, -1).start()

    outs = [pltpu.make_async_copy(mixed, mixed_hbm, out_sem.at[0])]
    outs[0].start()

    @pl.loop(0, NU)
    def _(unit):
        left = unpack(0, unit, 0, LANES - 6)
        part[unit] += back_short(0, gf0, q, gq, left, unit, tab[unit])

    turned = jnp.transpose(part[...].reshape(NU * rb, LANES))
    lane8 = lax.broadcasted_iota(jnp.int32, (8, LANES), 1)

    def moved(block, shift):
        return pltpu.roll(block, shift % LANES, 1) if shift % LANES else block

    for grp in range(S):
        base = grp * G // LANES * LANES
        tile = jnp.zeros((8, LANES), F32)
        for i in range(3):
            block = turned[8 * i : 8 * i + 8, base : base + LANES]
            tile = jnp.where(lane8 // G == i, moved(block, i * G - grp * G), tile)
        sums_send[grp] = tile
    sums_recv[me_s] = sums_send[me_s]

    def sums_copy(n, src, dst, t):
        return pltpu.make_async_remote_copy(
            src_ref=src, dst_ref=dst.at[me_s], send_sem=ssem.at[n], recv_sem=rsem.at[n],
            device_id=(t, me_c), device_id_type=MESH,
        )

    @pl.loop(1, S)
    def _(d):
        t = lax.rem(me_s + d, S)
        sums_copy(12, sums_send.at[t], sums_recv, t).start()

    each(lambda at: send_result(at, WAVES[1] + S, S + 1))

    for which in (2, 3):

        @pl.when(me_s < S - 1)
        def _():
            halo_copy(which, 1).wait_recv()

        @pl.when(me_s == S - 1)
        def _():
            halo_recv[which] = jnp.zeros(halo_recv.shape[1:], BF16)

    @pl.loop(0, NU)
    def _(unit):
        table = tab[unit]
        last_block(0, gf0, unpack(2, unit, 0, 0), gq, unit, table)
        last_block(1, gf1, unpack(3, unit, 0, 0), gk, unit, table)
        last_block(2, gf2, unpack(3, unit, 1, 0), gv, unit, table)

    for n, (src, dst) in enumerate(((gq, gq_hbm), (gk, gk_hbm), (gv, gv_hbm))):
        outs.append(pltpu.make_async_copy(src, dst, out_sem.at[n + 1]))
        outs[-1].start()

    take(12, sums_recv, S - 1)
    total = sums_recv[0]
    for s in range(1, S):
        total = total + sums_recv[s]
    total_send[...] = total * scale_root
    total_recv[me_s] = total_send[...]

    @pl.loop(1, S)
    def _(d):
        sums_copy(13, total_send, total_recv, lax.rem(me_s + d, S)).start()

    take(13, total_recv, S - 1)
    for base in range(0, S * G, LANES):
        for i in range(3):
            block = jnp.zeros((8, LANES), F32)
            for grp in range(base // G, min(S * G, base + LANES) // G):
                mine = lane8 // G == (grp * G - base) // G
                block = jnp.where(mine, moved(total_recv[grp], grp * G - i * G), block)
            short_out[i, :, base : base + LANES] = block[0:7]
            if i == 0:
                skip_out[:, base : base + LANES] = block[7:8]

    def all_sent(at):
        full, helps = plan.full[at], plan.help[at]
        early = at < A
        sent(0, filt_hbm, NU * H - full)
        sent(2, x_send, NU - full)
        sent(4, g_send, (na if early else NU) - full)
        sent(6, yf_send, (S if early else A) - 1, full)
        sent(8, bf_send, S - 1, full)
        sent(10, ff_send, S * H - 1, full)
        if early:
            sent(1, filt_hbm, nb * H - helps)
            sent(3, x_send, nb - helps)
            sent(5, g_send, nb - helps)
            sent(7, yh_send, A - 1, helps)
            sent(9, bh_send, A - 1, helps)
            sent(11, fh_send, A * H - 1, helps)
        for copy in own_result(at):
            copy.wait()
        take(10, gf_hbm, H * NU - full)
        if early:
            take(11, gf_more_hbm, H * nb - helps)

    sent(12, sums_recv, S - 1)
    sent(13, total_recv, S - 1)

    @pl.when(me_s < S - 1)
    def _():
        halo_copy(0, 1).wait_send()

    for which in (2, 3):

        @pl.when(me_s > 0)
        def _():
            halo_copy(which, -1).wait_send()

    for copy in outs:
        copy.wait()
    each(all_sent)


def hand_on(plan, arrays, more):
    pieces = [1 if a.size > 2**17 else 1 for a in arrays]
    count = len(arrays)
    parts = [a.shape[0] // cuts for a, cuts in zip(arrays, pieces)]
    H, NU, na, nb = plan.H, plan.NU, plan.na, plan.nb

    def body(*refs):
        sources, more_ref, dests = refs[:count], refs[count], refs[count + 1 : 2 * count + 1]
        held = refs[2 * count + 1 : 3 * count + 1]
        more_held, sem_in, sem_out, sem_more = refs[3 * count + 1 :]
        arriving, leaving = [], []
        order = [count - 1] + list(range(count - 1))
        for i in order:
            for at in range(pieces[i]):
                where = pl.ds(at * parts[i], parts[i])
                n = len(arriving)
                arriving.append(
                    pltpu.make_async_copy(sources[i].at[where], held[i].at[where], sem_in.at[n])
                )
                leaving.append(
                    pltpu.make_async_copy(held[i].at[where], dests[i].at[where], sem_out.at[n])
                )
        first_half = lax.axis_index("seq") < plan.A
        extra = pltpu.make_async_copy(more_ref, more_held, sem_more)

        @pl.when(first_half)
        def _():
            extra.start()

        for copy in arriving:
            copy.start()
        last = pieces[-1]
        for one, two in zip(arriving[last:], leaving[last:]):
            one.wait()
            two.start()
        for one in arriving[:last]:
            one.wait()

        @pl.when(first_half)
        def _():
            extra.wait()
            for c in range(H):

                @pl.loop(0, nb)
                def _(i):
                    total = held[-1][c * NU + na + i].astype(F32) + more_held[c * nb + i].astype(F32)
                    held[-1][c * NU + na + i] = total.astype(BF16)

        for two in leaving[:last]:
            two.start()
        for copy in leaving:
            copy.wait()

    spec = pl.BlockSpec(memory_space=pl.ANY)
    return pl.pallas_call(
        body,
        out_shape=tuple(jax.ShapeDtypeStruct(a.shape, a.dtype) for a in arrays),
        in_specs=[spec] * (count + 1),
        out_specs=(spec,) * count,
        scratch_shapes=[pltpu.VMEM(a.shape, a.dtype) for a in arrays + (more,)]
        + [pltpu.SemaphoreType.DMA((sum(pieces),))] * 2
        + [pltpu.SemaphoreType.DMA],
        compiler_params=pltpu.CompilerParams(vmem_limit_bytes=58 * 2**20),
    )(*arrays, more)


def per_device(query_proj, key_proj, value_proj, short_taps, skip_gain, filter_raw, grad_out):
    channels, T = query_proj.shape
    S = lax.axis_size("seq")
    H = lax.axis_size("chan")
    plan = Plan(S, H, channels, S * T)
    A, NU, rb, FT, nf, nh, nb = plan.A, plan.NU, plan.rb, plan.FT, plan.nf, plan.nh, plan.nb
    half = S * T // LANES
    split = lambda a: a.reshape(NU, rb, T)
    first, last, cols, cols_back, twist, twist_back = make_tables(S * T, S * T)
    first_h, last_h, _, _, twist_h, twist_back_h = make_tables(A * T, S * T)
    tables = (first, last, twist, twist_back, first_h, last_h, twist_h, twist_back_h, cols, cols_back)
    any_spec = pl.BlockSpec(memory_space=pl.ANY)
    vmem = pl.BlockSpec(memory_space=pltpu.VMEM)
    stream = jax.ShapeDtypeStruct((NU, rb, T), BF16)
    held = pltpu.VMEM((NU, rb, T), BF16)
    wide = pltpu.VMEM((NU, rb, T), F32)
    edge = pltpu.VMEM((4, NU // 8, rb, LANES), BF16)
    small = pltpu.VMEM((NU, rb, LANES), F32)
    outs = pl.pallas_call(
        functools.partial(kernel, plan),
        out_shape=(
            stream, stream, stream, stream,
            jax.ShapeDtypeStruct((3, 7, channels), F32),
            jax.ShapeDtypeStruct((1, channels), F32),
            jax.ShapeDtypeStruct((H * NU, rb, FT), BF16),
            jax.ShapeDtypeStruct((H * nb, rb, FT), BF16),
        ),
        in_specs=[any_spec] * 4 + [vmem] * 2 + [any_spec] + [(any_spec,) * len(tables)],
        out_specs=(any_spec,) * 4 + (vmem,) * 2 + (any_spec,) * 2,
        scratch_shapes=[
            tuple(pltpu.VMEM(a.shape, a.dtype) for a in tables),
            held, held, held, held,
            pltpu.VMEM((LANES, channels), F32),
            small, small,
            held, wide, wide,
            edge, edge,
            held, held,
            pltpu.VMEM((S * H, nf, rb, FT), BF16),
            pltpu.VMEM((S, nf, rb, T), BF16),
            pltpu.VMEM((S, nf, rb, T), BF16),
            pltpu.VMEM((A * H, nh, rb, FT), BF16),
            pltpu.VMEM((A, nh, rb, T), BF16),
            pltpu.VMEM((A, nh, rb, T), BF16),
            pltpu.VMEM((half * rb, LANES), F32),
            pltpu.VMEM((3, nf * rb, half, 2 * LANES), BF16),
            pltpu.VMEM((3, nh * rb, half // 2, 2 * LANES), BF16),
            pltpu.VMEM((S, nf, rb, T), BF16),
            pltpu.VMEM((S, nf, rb, T), BF16),
            pltpu.VMEM((S * H, nf, rb, FT), BF16),
            pltpu.VMEM((A, nh, rb, T), BF16),
            pltpu.VMEM((A, nh, rb, T), BF16),
            pltpu.VMEM((A * H, nh, rb, FT), BF16),
            held, held, held,
            held, held, held,
            held, held, held, held,
            pltpu.VMEM((S, 8, LANES), F32),
            pltpu.VMEM((S, 8, LANES), F32),
            pltpu.VMEM((8, LANES), F32),
            pltpu.VMEM((S, 8, LANES), F32),
            pltpu.SemaphoreType.DMA((len(tables),)),
            pltpu.SemaphoreType.DMA((4,)),
            pltpu.SemaphoreType.DMA((4,)),
            pltpu.SemaphoreType.DMA((4,)),
            pltpu.SemaphoreType.DMA((4,)),
            pltpu.SemaphoreType.DMA((4,)),
            pltpu.SemaphoreType.DMA((14,)),
            pltpu.SemaphoreType.DMA((14,)),
        ],
        compiler_params=pltpu.CompilerParams(
            collective_id=0, has_side_effects=True, vmem_limit_bytes=60 * 2**20
        ),
        cost_estimate=pl.CostEstimate(
            flops=6 * 4 * channels * T * S * 16, bytes_accessed=12 * channels * T * 2, transcendentals=0
        ),
    )(
        split(query_proj), split(key_proj), split(value_proj), split(grad_out),
        short_taps, skip_gain.reshape(1, channels), filter_raw.reshape(H * NU, rb, FT),
        tables,
    )
    mixed, gq, gk, gv, short, skip, gf = hand_on(plan, outs[:-1], outs[-1])
    back = lambda a: a.reshape(channels, T)
    return (
        back(mixed), back(gq), back(gk), back(gv), short, skip.reshape(channels),
        gf.reshape(H * NU * rb, FT),
    )


def solution(mesh):
    placed = (
        P("chan", "seq"),
        P("chan", "seq"),
        P("chan", "seq"),
        P(None, None, "chan"),
        P("chan"),
        P(None, ("seq", "chan")),
        P("chan", "seq"),
    )
    return jax.shard_map(
        per_device,
        mesh=mesh,
        in_specs=placed,
        out_specs=(
            P("chan", "seq"),
            P("chan", "seq"),
            P("chan", "seq"),
            P("chan", "seq"),
            P(None, None, "chan"),
            P("chan"),
            P(None, ("seq", "chan")),
        ),
        check_vma=False,
    )
```
